32 devices in a mesh: space: 8 (over z, x), tm: 4 (over y, core).
Axes of the slice: x: 2, y: 2, z: 4, core: 2. Of those that a mesh axis runs over, the one named last changes fastest.
Arguments:
- field: bfloat16 [1024, 196608], P('tm', 'space'), may hold values from -6 to 6
- temporal_cov: bfloat16 [1024, 1024], replicated
- spatial_blocks: bfloat16 [1536, 9, 128, 128], P(('space', 'tm')), may hold values from -0.3125 to 0.3125
- neighbours: int32 [1536, 9], P(('space', 'tm')), may hold values from -4 to 1539, as said below
- counts: int32 [1536], P(('space', 'tm')), may hold values from 1 to 9, as said below
Outputs:
- covariant_field: bfloat16 [1024, 196608], P('tm', 'space')
The draws below stay inside these ranges and needn't reach their ends.
Inputs may be any that keep to these rules, and one draw needn't show every extreme that they name: `neighbours`: row b holds b + o for every o from -4 to 4, each once, in an order drawn for each row; values outside 0 to 1535 name blocks of zeros. counts[b] is the number of leading slots of row b that are used.
All inputs are finite; a program needn't handle non-finite values.
Results may differ from the reference program's by a relative error of at most 0.005.
Values may be sent and summed in bfloat16 or wider, within the bound.
No kernel may reach another device: no remote copies, remote signals or barrier semaphores. Data moves between devices by JAX's collectives and lax.ppermute only.
A program may use at most 512 MiB of HBM per device.

```python
import math
import jax
import jax.numpy as jnp
from jax import lax

HOURS = 1024
BLOCK = 128
HB = 4
KMAX = 9
BLK_DEV = 192
NBLK = 1536
NCELL = 196608


def draw_temporal_cov(key, part):
    hours_axis = jnp.arange(HOURS, dtype=jnp.float32)
    distance = jnp.abs(hours_axis[:, None] - hours_axis[None, :])
    factor = jax.random.uniform(key, (HOURS, HOURS), jnp.float32, 0.25, 1.75)
    factor = 0.5 * (factor + factor.T)
    kernel_scale = 1.2 / math.sqrt(HOURS)
    matrix = jnp.eye(HOURS, dtype=jnp.float32) + kernel_scale * jnp.exp(-distance / (0.5 * HOURS)) * factor
    return matrix.astype(jnp.bfloat16)


def draw_neighbours(key, part):
    offset_count = 2 * HB + 1
    scores = jax.random.randint(key, (NBLK, offset_count), 0, 1 << 20)
    scores = scores * offset_count + jnp.arange(offset_count, dtype=jnp.int32)[None, :]
    offset_order = jnp.argsort(scores, axis=1).astype(jnp.int32)
    return (jnp.arange(NBLK, dtype=jnp.int32)[:, None] + offset_order - HB).astype(jnp.int32)


def draw_counts(key, part):
    region_key, slot_key, spot_key = jax.random.split(key, 3)
    regions = NBLK // BLK_DEV
    ceiling = jax.random.randint(region_key, (regions,), 2, KMAX + 1)
    per_block = jnp.repeat(ceiling, BLK_DEV)
    drawn_counts = jax.random.randint(slot_key, (NBLK,), 1, per_block + 1)
    full_spot = jax.random.randint(spot_key, (), 0, NBLK)
    return jnp.where(jnp.arange(NBLK, dtype=jnp.int32) == full_spot, KMAX, drawn_counts).astype(jnp.int32)


def level_of(key, shape, shards, least, high):
    gain = 1.0
    for position, shards_of in shards:
        draws = jax.random.uniform(jax.random.fold_in(jax.random.fold_in(key, 6), position), (shards_of,), jnp.float32, least / len(shards), high / len(shards))
        gain = gain * jnp.repeat(jnp.exp(draws), shape[position] // shards_of).reshape((-1,) + (1,) * (len(shape) - 1 - position))
    return gain


def scatter_about(stream_key, dims, spread, bound, cuts=(), held_as=jnp.bfloat16):
    entries = jax.random.normal(stream_key, dims, jnp.float32) * spread
    if len(cuts) > 0:
        entries = level_of(stream_key, dims, cuts, -0.22, 0.18) * entries
    return jnp.clip(entries, min=-bound, max=bound).astype(held_as)


def setup_inputs(seed: int = 0) -> dict:
    key_list = jax.random.split(jax.random.key(seed), 6)
    field = scatter_about(key_list[0], (HOURS, NCELL), 1.0, 6.0, ((0, 4), (1, 8)))
    temporal_cov = draw_temporal_cov(jax.random.fold_in(key_list[5], 71), 0)
    spatial_blocks = scatter_about(key_list[2], (NBLK, KMAX, BLOCK, BLOCK), (3 * BLOCK) ** -0.5, 0.3125, ((0, 32),))
    neighbours = draw_neighbours(jax.random.fold_in(key_list[5], 71), 0)
    counts = draw_counts(jax.random.fold_in(key_list[5], 71), 0)
    return {"field": field, "temporal_cov": temporal_cov, "spatial_blocks": spatial_blocks, "neighbours": neighbours, "counts": counts}


def reference(field, temporal_cov, spatial_blocks, neighbours, counts):
    group_size = 16
    group_count = NBLK // group_size
    columns = field.reshape(HOURS, group_count, group_size * BLOCK).transpose(1, 0, 2)

    def temporal(panel):
        return jnp.dot(temporal_cov, panel, preferred_element_type=jnp.float32).astype(jnp.bfloat16)

    mixed_groups = lax.map(temporal, columns)
    temporal_mix = mixed_groups.transpose(1, 0, 2).reshape(HOURS, NBLK, BLOCK)
    padded = jnp.pad(temporal_mix, ((0, 0), (HB, HB), (0, 0)))
    live_slot = jnp.arange(KMAX, dtype=jnp.int32)[None, :] < counts[:, None]
    weights = jnp.where(live_slot[:, :, None, None], spatial_blocks, jnp.zeros((), spatial_blocks.dtype))
    positions = (neighbours + HB).astype(jnp.int32)

    def spatial(operands):
        spot_list, tile_set = operands
        picked = jnp.take(padded, spot_list.reshape(-1), axis=1).reshape(HOURS, group_size, KMAX, BLOCK)
        summed = jnp.einsum("tbkj,bkij->tbi", picked.astype(jnp.float32), tile_set.astype(jnp.float32))
        return summed.astype(jnp.bfloat16)

    outputs = lax.map(spatial, (positions.reshape(group_count, group_size, KMAX),
                                weights.reshape(group_count, group_size, KMAX, BLOCK, BLOCK)))
    return outputs.transpose(1, 0, 2, 3).reshape(HOURS, NCELL)
```

```python
import functools

import jax
import jax.numpy as jnp
from jax import lax
from jax.experimental import pallas as pl
from jax.experimental.pallas import tpu as pltpu
from jax.sharding import PartitionSpec as P

CHUNK_UNITS = 3
MiB = 1 << 20


def pack_kernel(place_ref, *refs):
    half = len(refs) // 2
    for source, target in zip(refs[:half], refs[half:]):
        target[...] = source[...]


def pack(field, place, peers, unit, group_units, first, count):
    hours_dev = field.shape[0]

    def source(peer):
        return pl.BlockSpec(
            (hours_dev, unit), lambda i, place: (0, place[peer] * group_units + first + i)
        )

    return pl.pallas_call(
        pack_kernel,
        out_shape=[jax.ShapeDtypeStruct((hours_dev, count * unit), field.dtype) for _ in peers],
        grid_spec=pltpu.PrefetchScalarGridSpec(
            num_scalar_prefetch=1,
            grid=(count,),
            in_specs=[source(peer) for peer in peers],
            out_specs=[pl.BlockSpec((hours_dev, unit), lambda i, place: (0, i)) for _ in peers],
        ),
        cost_estimate=pl.CostEstimate(
            flops=0,
            transcendentals=0,
            bytes_accessed=4 * len(peers) * hours_dev * count * unit,
        ),
        name="pack",
    )(place, *([field] * len(peers)))


def rim_kernel(groups, place_ref, low_ref, high_ref, *refs):
    half = len(refs) // 2
    side = pl.program_id(0)
    for peer, (source, target) in enumerate(zip(refs[:half], refs[half:])):
        group = place_ref[peer]

        @pl.when(side == 0)
        def _():
            target[...] = jnp.where(group == 0, low_ref[...], source[...])

        @pl.when(side == 1)
        def _():
            target[...] = jnp.where(group == groups - 1, high_ref[...], source[...])


def pack_rims(field, low, high, place, groups, unit, group_units):
    hours_dev = field.shape[0]
    last = groups * group_units - 1

    def source(peer):
        def index(side, place):
            first = place[peer] * group_units
            at = jnp.where(side == 0, first - 1, first + group_units)
            return 0, jnp.clip(at, 0, last)

        return pl.BlockSpec((hours_dev, unit), index)

    whole = pl.BlockSpec((hours_dev, unit), lambda side, place: (0, 0))
    return pl.pallas_call(
        functools.partial(rim_kernel, groups),
        out_shape=[
            jax.ShapeDtypeStruct((hours_dev, 2 * unit), field.dtype) for _ in range(groups)
        ],
        grid_spec=pltpu.PrefetchScalarGridSpec(
            num_scalar_prefetch=1,
            grid=(2,),
            in_specs=[whole, whole] + [source(peer) for peer in range(groups)],
            out_specs=[
                pl.BlockSpec((hours_dev, unit), lambda side, place: (0, side))
                for _ in range(groups)
            ],
        ),
        cost_estimate=pl.CostEstimate(
            flops=0, transcendentals=0, bytes_accessed=8 * groups * hours_dev * unit
        ),
        name="rims",
    )(place, low, high, *([field] * groups))


def rows_kernel(place_ref, source, target):
    target[...] = source[...]


def order_rows(temporal_cov, place, groups):
    hours_all = temporal_cov.shape[0]
    hours_dev = hours_all // groups
    return pl.pallas_call(
        rows_kernel,
        out_shape=jax.ShapeDtypeStruct(temporal_cov.shape, temporal_cov.dtype),
        grid_spec=pltpu.PrefetchScalarGridSpec(
            num_scalar_prefetch=1,
            grid=(groups,),
            in_specs=[pl.BlockSpec((hours_dev, hours_all), lambda i, place: (place[i], 0))],
            out_specs=pl.BlockSpec((hours_dev, hours_all), lambda i, place: (i, 0)),
        ),
        name="order",
    )(place, temporal_cov)


def product_kernel(cfg, place_ref, neighbours_ref, counts_ref, cov_ref, *refs):
    groups, unit, block, slots, steps, lead, first_out = cfg["dims"]
    has_low, has_high, has_carry, has_next = cfg["flags"]
    refs = list(refs)
    pieces = [refs.pop(0) for _ in range(groups)]
    rims = [refs.pop(0) for _ in range(groups)] if has_low or has_high else None
    carry_ref = refs.pop(0) if has_carry else None
    tiles_ref = refs.pop(0)
    outs = [refs.pop(0) for _ in range(groups)]
    next_ref = refs.pop(0) if has_next else None
    panel, mixed, banded = refs

    step = pl.program_id(0)
    hours_dev = pieces[0].shape[0]
    reach = (slots - 1) // 2
    width = slots + 1

    @pl.when(step == 0)
    def _():
        for pair in range(banded.shape[0]):
            banded[pair, :block, slots * block :] = jnp.zeros((block, block), banded.dtype)
            banded[pair, block:, :block] = jnp.zeros((block, block), banded.dtype)
        if has_carry:
            mixed[:, : 2 * unit] = carry_ref[...]

    def load(sources):
        for peer in range(groups):
            at = pl.multiple_of(place_ref[peer] * hours_dev, hours_dev)
            panel[pl.ds(at, hours_dev), :] = sources[peer][...]

    if has_low or has_high:
        at_rim = jnp.bool_(False)
        if has_low:
            at_rim = jnp.logical_or(at_rim, step == 0)
        if has_high:
            at_rim = jnp.logical_or(at_rim, step == steps - 1)

        @pl.when(at_rim)
        def _():
            load(rims)

        @pl.when(jnp.logical_not(at_rim))
        def _():
            load(pieces)
    else:
        load(pieces)

    fresh = jnp.dot(cov_ref[...], panel[...], preferred_element_type=jnp.float32).astype(mixed.dtype)
    mixed[:, pl.ds(pl.multiple_of((step + lead) * unit, unit), unit)] = fresh
    if has_next:
        for which in range(2):

            @pl.when(step == steps - 2 + which)
            def _():
                next_ref[:, which * unit : (which + 1) * unit] = fresh

    @pl.when(step + lead >= 2)
    def _():
        out_unit = step + lead - 2
        first_row = (first_out + out_unit) * (unit // block)
        base = pl.multiple_of(out_unit * unit, unit)
        for pair in range(unit // block // 2):
            for which in range(2):
                row = 2 * pair + which
                mine = first_row + row
                block_id = place_ref[groups] + mine
                live = counts_ref[mine]
                for slot in range(slots):
                    offset = neighbours_ref[mine, slot] - block_id + (reach + which)
                    offset = jnp.clip(offset, 0, slots)
                    tile = tiles_ref[row, slot]
                    banded[
                        pair,
                        which * block : (which + 1) * block,
                        pl.ds(pl.multiple_of(offset * block, block), block),
                    ] = jnp.where(slot < live, tile, jnp.zeros_like(tile))
            window = mixed[:, pl.ds(pl.multiple_of(base + 2 * pair * block, block), width * block)]
            summed = lax.dot_general(
                window, banded[pair], (((1,), (1,)), ((), ())), preferred_element_type=jnp.float32
            ).astype(outs[0].dtype)
            for peer in range(groups):
                outs[peer][:, 2 * pair * block : 2 * (pair + 1) * block] = summed[
                    peer * hours_dev : (peer + 1) * hours_dev
                ]


def products(
    place, neighbours, counts, cov, field, pieces, rims, carry, spatial_blocks, layout, chunk
):
    groups, unit, block, slots, group_units, chunk_units = layout
    chunks = group_units // chunk_units
    hours_all, hours_dev = cov.shape[0], field.shape[0]
    has_low, has_high = chunk == 0, chunk == chunks - 1
    has_carry, has_next = chunk > 0, chunk < chunks - 1
    lead = 2 if has_carry else 0
    steps = chunk_units + 2 - lead
    first_out = chunk * chunk_units
    first_main = 0 if has_low else first_out + 1
    main_count = steps - int(has_low) - int(has_high)
    skip = int(has_low)

    def main(i):
        return jnp.clip(i - skip, 0, main_count - 1)

    own_spec = pl.BlockSpec(
        (hours_dev, unit), lambda i, place, *_: (0, place[0] * group_units + first_main + main(i))
    )
    piece_spec = pl.BlockSpec((hours_dev, unit), lambda i, *_: (0, main(i)))

    def rim_index(i, *_):
        if has_low and has_high:
            return 0, jnp.where(i == 0, 0, 1)
        return 0, (0 if has_low else 1)

    def out_unit(i):
        return jnp.maximum(i + lead - 2, 0)

    blocks_unit = unit // block
    in_specs = [pl.BlockSpec((hours_all, hours_all), lambda i, *_: (0, 0))]
    in_specs += [own_spec] + [piece_spec] * (groups - 1)
    operands = [cov, field] + list(pieces)
    if has_low or has_high:
        in_specs += [pl.BlockSpec((hours_dev, unit), rim_index)] * groups
        operands += list(rims)
    if has_carry:
        in_specs += [pl.BlockSpec((hours_all, 2 * unit), lambda i, *_: (0, 0))]
        operands += [carry]
    in_specs += [
        pl.BlockSpec(
            (blocks_unit, slots, block, block), lambda i, *_: (first_out + out_unit(i), 0, 0, 0)
        )
    ]
    operands += [spatial_blocks]
    out_shape = [
        jax.ShapeDtypeStruct((hours_dev, chunk_units * unit), field.dtype) for _ in range(groups)
    ]
    out_specs = [pl.BlockSpec((hours_dev, unit), lambda i, *_: (0, out_unit(i)))] * groups
    if has_next:
        out_shape += [jax.ShapeDtypeStruct((hours_all, 2 * unit), field.dtype)]
        out_specs += [pl.BlockSpec((hours_all, 2 * unit), lambda i, *_: (0, 0))]
    cfg = {
        "dims": (groups, unit, block, slots, steps, lead, first_out),
        "flags": (has_low, has_high, has_carry, has_next),
    }
    flops = 2 * hours_all * unit * (steps * hours_all + chunk_units * (slots + 1) * block)
    results = pl.pallas_call(
        functools.partial(product_kernel, cfg),
        out_shape=out_shape,
        grid_spec=pltpu.PrefetchScalarGridSpec(
            num_scalar_prefetch=3,
            grid=(steps,),
            in_specs=in_specs,
            out_specs=out_specs,
            scratch_shapes=[
                pltpu.VMEM((hours_all, unit), field.dtype),
                pltpu.VMEM((hours_all, (chunk_units + 2) * unit), field.dtype),
                pltpu.VMEM((blocks_unit // 2, 2 * block, (slots + 1) * block), field.dtype),
            ],
        ),
        compiler_params=pltpu.CompilerParams(vmem_limit_bytes=48 * MiB),
        cost_estimate=pl.CostEstimate(
            flops=flops,
            transcendentals=0,
            bytes_accessed=2 * hours_all * unit * (steps + chunk_units)
            + 2 * chunk_units * blocks_unit * slots * block * block,
        ),
        name="products",
    )(place, neighbours, counts, *operands)
    return results[:groups], (results[groups] if has_next else None)


def place_kernel(groups, place_ref, *refs):
    target = refs[-1]
    which = pl.program_id(0)
    for peer in range(groups):

        @pl.when(which == peer)
        def _():
            target[...] = refs[peer][...]


def put(result, pieces, place, cells_dev, unit, group_units, first_out):
    groups = len(pieces)
    hours_dev, columns = pieces[0].shape
    count = columns // unit

    def piece_spec(peer):
        def index(which, i, place):
            return 0, jnp.where(which == peer, i, jnp.where(which < peer, 0, count - 1))

        return pl.BlockSpec((hours_dev, unit), index)

    in_specs = [piece_spec(peer) for peer in range(groups)]
    operands = list(pieces)
    aliases = {}
    if result is not None:
        in_specs += [pl.BlockSpec(memory_space=pl.ANY)]
        operands += [result]
        aliases = {1 + groups: 0}
    return pl.pallas_call(
        functools.partial(place_kernel, groups),
        out_shape=jax.ShapeDtypeStruct((hours_dev, cells_dev), pieces[0].dtype),
        grid_spec=pltpu.PrefetchScalarGridSpec(
            num_scalar_prefetch=1,
            grid=(groups, count),
            in_specs=in_specs,
            out_specs=pl.BlockSpec(
                (hours_dev, unit),
                lambda which, i, place: (0, place[which] * group_units + first_out + i),
            ),
        ),
        input_output_aliases=aliases,
        cost_estimate=pl.CostEstimate(
            flops=0, transcendentals=0, bytes_accessed=4 * groups * hours_dev * columns
        ),
        name="place",
    )(place, *operands)


def per_device(field, temporal_cov, spatial_blocks, neighbours, counts):
    groups = lax.axis_size("tm")
    spaces = lax.axis_size("space")
    hours_dev, cells_dev = field.shape
    per_group, slots, block = spatial_blocks.shape[:3]
    reach = (slots - 1) // 2
    unit = reach * block
    group_units = per_group // reach
    chunk_units = CHUNK_UNITS if group_units % CHUNK_UNITS == 0 else group_units
    chunks = group_units // chunk_units
    layout = (groups, unit, block, slots, group_units, chunk_units)

    mine = lax.axis_index("tm")
    first_block = (lax.axis_index("space") * groups + mine) * per_group
    place = jnp.concatenate(
        [
            jnp.bitwise_xor(mine.astype(jnp.int32), jnp.arange(groups, dtype=jnp.int32)),
            first_block.astype(jnp.int32)[None],
        ]
    )

    def swap(array, peer):
        return lax.ppermute(array, "tm", [(at, at ^ peer) for at in range(groups)])

    peers = list(range(1, groups))
    far_first = peers[::-1]

    def swap_all(arrays):
        moved = {peer: swap(arrays[peer - 1], peer) for peer in far_first}
        return [moved[peer] for peer in peers]

    forward = [(at, at + 1) for at in range(spaces - 1)]
    backward = [(to, at) for at, to in forward]

    spans = []
    for chunk in range(chunks):
        start = 0 if chunk == 0 else chunk * chunk_units + 1
        stop = group_units if chunk == chunks - 1 else (chunk + 1) * chunk_units + 1
        spans.append((start, stop - start))

    sent = pack(field, place, peers, unit, group_units, *spans[0])
    arrived = [swap_all(sent)]
    low = lax.ppermute(field[:, cells_dev - unit :], "space", forward)
    high = lax.ppermute(field[:, :unit], "space", backward)
    rims_out = pack_rims(field, low, high, place, groups, unit, group_units)
    rims = [rims_out[0]] + swap_all(rims_out[1:])
    for chunk in range(1, chunks):
        arrived.append(swap_all(pack(field, place, peers, unit, group_units, *spans[chunk])))

    cov = order_rows(temporal_cov, place, groups)
    carry, result = None, None
    returned = []
    for chunk in range(chunks):
        outs, carry = products(
            place, neighbours, counts, cov, field, arrived[chunk], rims, carry,
            spatial_blocks, layout, chunk,
        )
        returned.append([outs[0]] + swap_all(outs[1:]))
    for chunk in range(chunks):
        result = put(
            result, returned[chunk], place, cells_dev, unit, group_units, chunk * chunk_units
        )
    return result


def solution(mesh):
    placed = (
        P("tm", "space"),
        P(),
        P(("space", "tm"), None, None, None),
        P(("space", "tm"), None),
        P(("space", "tm")),
    )
    return jax.shard_map(
        per_device, mesh=mesh, in_specs=placed, out_specs=P("tm", "space"), check_vma=False
    )
```

```python
import functools

import jax
import jax.numpy as jnp
from jax import lax
from jax.experimental import pallas as pl
from jax.experimental.pallas import tpu as pltpu
from jax.sharding import PartitionSpec as P


CHUNK_UNITS = 3
MiB = 1 << 20


def ascends(group):
    return jnp.bitwise_and(group, 1) == 1


def pack_kernel(last, sources, place_ref, *refs):
    inputs, targets = refs[: -len(sources)], refs[-len(sources) :]
    low_ref, high_ref = inputs[len(sources) :] if len(inputs) > len(sources) else (None, None)
    for peer, target in enumerate(targets):
        value = inputs[peer][...]
        if low_ref is not None:
            at = sources[peer](pl.program_id(0), place_ref)
            value = jnp.where(at < 0, low_ref[...], jnp.where(at > last, high_ref[...], value))
        target[...] = value


def pack(field, place, halo, peers, unit, group_units, first, count, groups):
    hours_dev = field.shape[0]
    last = groups * group_units - 1

    def source_of(peer):
        def source(i, place):
            group = place[peer]
            start = jnp.where(ascends(group), first, group_units - first - count)
            return group * group_units + start + i

        return source

    sources = [source_of(peer) for peer in peers]

    def spec(source):
        return pl.BlockSpec(
            (hours_dev, unit), lambda i, place: (0, jnp.clip(source(i, place), 0, last))
        )

    in_specs = [spec(source) for source in sources]
    operands = [field] * len(peers)
    if halo is not None:
        in_specs += [pl.BlockSpec((hours_dev, unit), lambda i, place: (0, 0))] * 2
        operands += list(halo)
    return pl.pallas_call(
        functools.partial(pack_kernel, last, sources),
        out_shape=[jax.ShapeDtypeStruct((hours_dev, count * unit), field.dtype) for _ in peers],
        grid_spec=pltpu.PrefetchScalarGridSpec(
            num_scalar_prefetch=1,
            grid=(count,),
            in_specs=in_specs,
            out_specs=[pl.BlockSpec((hours_dev, unit), lambda i, place: (0, i)) for _ in peers],
        ),
        cost_estimate=pl.CostEstimate(
            flops=0,
            transcendentals=0,
            bytes_accessed=4 * len(peers) * hours_dev * count * unit,
        ),
        name="pack",
    )(place, *operands)


def rows_kernel(place_ref, source, target):
    target[...] = source[...]


def order_rows(temporal_cov, place, groups):
    hours_all = temporal_cov.shape[0]
    hours_dev = hours_all // groups
    return pl.pallas_call(
        rows_kernel,
        out_shape=jax.ShapeDtypeStruct(temporal_cov.shape, temporal_cov.dtype),
        grid_spec=pltpu.PrefetchScalarGridSpec(
            num_scalar_prefetch=1,
            grid=(groups,),
            in_specs=[pl.BlockSpec((hours_dev, hours_all), lambda i, place: (place[i], 0))],
            out_specs=pl.BlockSpec((hours_dev, hours_all), lambda i, place: (i, 0)),
        ),
        name="order",
    )(place, temporal_cov)


def product_kernel(cfg, place_ref, neighbours_ref, counts_ref, cov_ref, *refs):
    groups, unit, block, slots, chunk_units, group_units, first_out, lead = cfg["dims"]
    opening, has_next = cfg["flags"]
    refs = list(refs)
    pieces = [refs.pop(0) for _ in range(groups)]
    inner = [refs.pop(0) for _ in range(groups)] if opening else None
    outset = [refs.pop(0) for _ in range(groups)] if opening else None
    carry_ref = None if opening else refs.pop(0)
    tiles_ref = refs.pop(0)
    outs = [refs.pop(0) for _ in range(groups)]
    next_ref = refs.pop(0) if has_next else None
    panel, mixed, banded = refs

    step = pl.program_id(0)
    steps = pl.num_programs(0)
    upward = ascends(place_ref[0])
    hours_dev = pieces[0].shape[0]
    reach = (slots - 1) // 2
    width = slots + 1

    def columns(position):
        at = jnp.where(upward, position, chunk_units + 1 - position)
        return pl.ds(pl.multiple_of(at * unit, unit), unit)

    @pl.when(step == 0)
    def _():
        for pair in range(banded.shape[0]):
            banded[pair, :block, slots * block :] = jnp.zeros((block, block), banded.dtype)
            banded[pair, block:, :block] = jnp.zeros((block, block), banded.dtype)
        if not opening:
            for which in range(2):
                mixed[:, columns(which)] = carry_ref[:, which * unit : (which + 1) * unit]

    def load(sources):
        for peer in range(groups):
            at = pl.multiple_of(place_ref[peer] * hours_dev, hours_dev)
            panel[pl.ds(at, hours_dev), :] = sources[peer][...]

    if opening:
        pl.when(step == 0)(lambda: load(inner))
        pl.when(step == 1)(lambda: load(outset))
        pl.when(step >= 2)(lambda: load(pieces))
    else:
        load(pieces)

    fresh = jnp.dot(cov_ref[...], panel[...], preferred_element_type=jnp.float32).astype(mixed.dtype)
    mixed[:, columns(step + lead)] = fresh
    if has_next:
        for which in range(2):

            @pl.when(step == steps - 2 + which)
            def _():
                next_ref[:, which * unit : (which + 1) * unit] = fresh

    @pl.when(step + lead >= 2)
    def _():
        turn = step + lead - 2
        at = jnp.where(upward, turn, chunk_units - 1 - turn)
        own_unit = jnp.where(upward, first_out + turn, group_units - 1 - first_out - turn)
        first_row = own_unit * (unit // block)
        base = pl.multiple_of(at * unit, unit)
        for pair in range(unit // block // 2):
            for which in range(2):
                row = 2 * pair + which
                mine = first_row + row
                block_id = place_ref[groups] + mine
                live = counts_ref[mine]
                for slot in range(slots):
                    offset = neighbours_ref[mine, slot] - block_id + (reach + which)
                    offset = jnp.clip(offset, 0, slots)
                    tile = tiles_ref[row, slot]
                    banded[
                        pair,
                        which * block : (which + 1) * block,
                        pl.ds(pl.multiple_of(offset * block, block), block),
                    ] = jnp.where(slot < live, tile, jnp.zeros_like(tile))
            window = mixed[:, pl.ds(pl.multiple_of(base + 2 * pair * block, block), width * block)]
            summed = lax.dot_general(
                window, banded[pair], (((1,), (1,)), ((), ())), preferred_element_type=jnp.float32
            ).astype(outs[0].dtype)
            for peer in range(groups):
                outs[peer][:, 2 * pair * block : 2 * (pair + 1) * block] = summed[
                    peer * hours_dev : (peer + 1) * hours_dev
                ]


def products(place, neighbours, counts, cov, pieces, start, carry, spatial_blocks, layout, chunk):
    groups, unit, block, slots, group_units, chunk_units = layout
    chunks = group_units // chunk_units
    hours_all, hours_dev = cov.shape[0], pieces[0].shape[0]
    opening, has_next = chunk == 0, chunk < chunks - 1
    lead = 0 if opening else 2
    steps = chunk_units + 2 - lead
    first_out = chunk * chunk_units

    def piece_index(i, place, *_):
        turn = jnp.maximum(i + lead - 2, 0)
        return 0, jnp.where(ascends(place[0]), turn, chunk_units - 1 - turn)

    def tile_index(i, place, *_):
        turn = first_out + jnp.maximum(i + lead - 2, 0)
        return jnp.where(ascends(place[0]), turn, group_units - 1 - turn), 0, 0, 0

    def whole(shape):
        return pl.BlockSpec(shape, lambda i, *_: (0, 0))

    piece_spec = pl.BlockSpec((hours_dev, unit), piece_index)
    in_specs = [whole((hours_all, hours_all))] + [piece_spec] * groups
    operands = [cov] + list(pieces)
    if opening:
        in_specs += [whole((hours_dev, unit))] * (2 * groups)
        operands += list(start[0]) + list(start[1])
    else:
        in_specs += [whole((hours_all, 2 * unit))]
        operands += [carry]
    blocks_unit = unit // block
    in_specs += [pl.BlockSpec((blocks_unit, slots, block, block), tile_index)]
    operands += [spatial_blocks]
    dtype = pieces[0].dtype
    out_shape = [jax.ShapeDtypeStruct((hours_dev, chunk_units * unit), dtype)] * groups
    out_specs = [piece_spec] * groups
    if has_next:
        out_shape += [jax.ShapeDtypeStruct((hours_all, 2 * unit), dtype)]
        out_specs += [whole((hours_all, 2 * unit))]
    cfg = {
        "dims": (groups, unit, block, slots, chunk_units, group_units, first_out, lead),
        "flags": (opening, has_next),
    }
    flops = 2 * hours_all * unit * (steps * hours_all + chunk_units * (slots + 1) * block)
    results = pl.pallas_call(
        functools.partial(product_kernel, cfg),
        out_shape=out_shape,
        grid_spec=pltpu.PrefetchScalarGridSpec(
            num_scalar_prefetch=3,
            grid=(steps,),
            in_specs=in_specs,
            out_specs=out_specs,
            scratch_shapes=[
                pltpu.VMEM((hours_all, unit), dtype),
                pltpu.VMEM((hours_all, (chunk_units + 2) * unit), dtype),
                pltpu.VMEM((blocks_unit // 2, 2 * block, (slots + 1) * block), dtype),
            ],
        ),
        compiler_params=pltpu.CompilerParams(vmem_limit_bytes=48 * MiB),
        cost_estimate=pl.CostEstimate(
            flops=flops,
            transcendentals=0,
            bytes_accessed=2 * hours_all * unit * (steps + chunk_units)
            + 2 * chunk_units * blocks_unit * slots * block * block,
        ),
        name="products",
    )(place, neighbours, counts, *operands)
    return results[:groups], (results[groups] if has_next else None)


def place_kernel(peers, chunks, chunk, place_ref, *refs):
    target, sems = refs[-2], refs[-1]
    copies = []
    for which, peer in enumerate(peers):
        source = refs[which]
        columns = source.shape[1]
        group = place_ref[peer]
        at = group * chunks + jnp.where(ascends(group), chunk, chunks - 1 - chunk)
        copies.append(
            pltpu.make_async_copy(
                source,
                target.at[:, pl.ds(pl.multiple_of(at * columns, columns), columns)],
                sems.at[which],
            )
        )
    for copy in copies:
        copy.start()
    for copy in copies:
        copy.wait()


def put(result, pieces, peers, place, cells_dev, chunks, chunk):
    hours_dev, columns = pieces[0].shape
    in_specs = [pl.BlockSpec(memory_space=pltpu.VMEM)] * len(pieces)
    operands = list(pieces)
    aliases = {}
    if result is not None:
        in_specs += [pl.BlockSpec(memory_space=pl.ANY)]
        operands += [result]
        aliases = {1 + len(pieces): 0}
    return pl.pallas_call(
        functools.partial(place_kernel, peers, chunks, chunk),
        out_shape=jax.ShapeDtypeStruct((hours_dev, cells_dev), pieces[0].dtype),
        grid_spec=pltpu.PrefetchScalarGridSpec(
            num_scalar_prefetch=1,
            grid=(),
            in_specs=in_specs,
            out_specs=pl.BlockSpec(memory_space=pl.ANY),
            scratch_shapes=[pltpu.SemaphoreType.DMA((len(pieces),))],
        ),
        input_output_aliases=aliases,
        cost_estimate=pl.CostEstimate(
            flops=0, transcendentals=0, bytes_accessed=4 * len(pieces) * hours_dev * columns
        ),
        name="place",
    )(place, *operands)


def per_device(field, temporal_cov, spatial_blocks, neighbours, counts):
    groups = lax.axis_size("tm")
    spaces = lax.axis_size("space")
    _, cells_dev = field.shape
    per_group, slots, block = spatial_blocks.shape[:3]
    reach = (slots - 1) // 2
    unit = reach * block
    group_units = per_group // reach
    chunk_units = CHUNK_UNITS if group_units % CHUNK_UNITS == 0 else group_units
    chunks = group_units // chunk_units
    layout = (groups, unit, block, slots, group_units, chunk_units)

    mine = lax.axis_index("tm")
    first_block = (lax.axis_index("space") * groups + mine) * per_group
    place = jnp.concatenate(
        [
            jnp.bitwise_xor(mine.astype(jnp.int32), jnp.arange(groups, dtype=jnp.int32)),
            first_block.astype(jnp.int32)[None],
        ]
    )

    def swap(array, peer):
        return lax.ppermute(array, "tm", [(at, at ^ peer) for at in range(groups)])

    def swap_all(arrays):
        moved = {peer: swap(arrays[peer], peer) for peer in range(groups - 1, 0, -1)}
        return [arrays[0]] + [moved[peer] for peer in range(1, groups)]

    forward = [(at, at + 1) for at in range(spaces - 1)]
    backward = [(to, at) for at, to in forward]
    peers = list(range(groups))

    first_sent = pack(field, place, None, peers, unit, group_units, 0, 1, groups)
    first = swap_all(first_sent)
    low = lax.ppermute(field[:, cells_dev - unit :], "space", forward)
    high = lax.ppermute(field[:, :unit], "space", backward)
    arrived, sent = [], first_sent
    for chunk in range(chunks):
        halo = (low, high) if chunk == chunks - 1 else None
        turn, _ = lax.optimization_barrier((place, sent[-1]))
        sent = pack(
            field, turn, halo, peers, unit, group_units,
            1 + chunk * chunk_units, chunk_units, groups,
        )
        arrived.append(swap_all(sent))
    inner = [first_sent[1]] + [swap(first[peer ^ 1], 1) for peer in range(1, groups)]
    cov = order_rows(temporal_cov, place, groups)
    carry, result = None, None
    returned = []
    for chunk in range(chunks):
        outs, carry = products(
            place, neighbours, counts, cov, arrived[chunk], (inner, first), carry,
            spatial_blocks, layout, chunk,
        )
        returned.append(swap_all(outs))
    for chunk in range(chunks):
        near, far = (peers, []) if chunk < chunks - 1 else (peers[:2], peers[2:])
        for listed in (near, far):
            if listed:
                result = put(
                    result, [returned[chunk][peer] for peer in listed], listed, place,
                    cells_dev, chunks, chunk,
                )
    return result


def solution(mesh):
    placed = (
        P("tm", "space"),
        P(),
        P(("space", "tm"), None, None, None),
        P(("space", "tm"), None),
        P(("space", "tm")),
    )
    return jax.shard_map(
        per_device, mesh=mesh, in_specs=placed, out_specs=P("tm", "space"), check_vma=False
    )
```

```python
import functools

import jax
import jax.numpy as jnp
from jax import lax
from jax.experimental import pallas as pl
from jax.experimental.pallas import tpu as pltpu
from jax.sharding import PartitionSpec as P


CHUNK_UNITS = 6
MiB = 1 << 20


def ascends(group):
    return jnp.bitwise_and(group, 1) == 1


def pack_kernel(last, sources, place_ref, *refs):
    inputs, targets = refs[: -len(sources)], refs[-len(sources) :]
    low_ref, high_ref = inputs[len(sources) :]
    for peer, target in enumerate(targets):
        at = sources[peer](pl.program_id(0), place_ref)
        target[...] = jnp.where(
            at < 0, low_ref[...], jnp.where(at > last, high_ref[...], inputs[peer][...])
        )


def copy_kernel(unit, sources, on_chip, place_ref, field_ref, *refs):
    count = len(sources)
    targets, sems = refs[:count], refs[-1]
    gathered = targets if on_chip else [refs[count].at[which] for which in range(count)]
    columns = targets[0].shape[1]
    reads, writes = [], []
    for which, source in enumerate(sources):
        at = pl.multiple_of(source(0, place_ref) * unit, unit)
        reads.append(
            pltpu.make_async_copy(
                field_ref.at[:, pl.ds(at, columns)], gathered[which], sems.at[0, which]
            )
        )
        if not on_chip:
            writes.append(
                pltpu.make_async_copy(gathered[which], targets[which], sems.at[1, which])
            )
    for read in reads:
        read.start()
    for which, read in enumerate(reads):
        read.wait()
        if writes:
            writes[which].start()
    for write in writes:
        write.wait()


def pack(field, place, halo, peers, unit, group_units, first, count, groups, on_chip=False):
    hours_dev = field.shape[0]
    last = groups * group_units - 1

    def source_of(peer):
        def source(i, place):
            group = place[peer]
            start = jnp.where(ascends(group), first, group_units - first - count)
            return group * group_units + start + i

        return source

    sources = [source_of(peer) for peer in peers]

    def spec(source):
        return pl.BlockSpec(
            (hours_dev, unit), lambda i, place: (0, jnp.clip(source(i, place), 0, last))
        )

    bytes_moved = 4 * len(peers) * hours_dev * count * unit
    if halo is None:
        shape = (hours_dev, count * unit)
        kind = pltpu.VMEM if on_chip else jax.ShapeDtypeStruct
        space = pltpu.VMEM if on_chip else pl.ANY
        scratch = [] if on_chip else [pltpu.VMEM((len(peers),) + shape, field.dtype)]
        return pl.pallas_call(
            functools.partial(copy_kernel, unit, sources, on_chip),
            out_shape=[kind(shape, field.dtype) for _ in peers],
            grid_spec=pltpu.PrefetchScalarGridSpec(
                num_scalar_prefetch=1,
                grid=(),
                in_specs=[pl.BlockSpec(memory_space=pl.ANY)],
                out_specs=[pl.BlockSpec(memory_space=space) for _ in peers],
                scratch_shapes=scratch + [pltpu.SemaphoreType.DMA((2, len(peers)))],
            ),
            cost_estimate=pl.CostEstimate(
                flops=0, transcendentals=0, bytes_accessed=bytes_moved
            ),
            name="pack",
        )(place, field)
    in_specs = [spec(source) for source in sources]
    operands = [field] * len(peers)
    in_specs += [pl.BlockSpec((hours_dev, unit), lambda i, place: (0, 0))] * 2
    operands += list(halo)
    return pl.pallas_call(
        functools.partial(pack_kernel, last, sources),
        out_shape=[jax.ShapeDtypeStruct((hours_dev, count * unit), field.dtype) for _ in peers],
        grid_spec=pltpu.PrefetchScalarGridSpec(
            num_scalar_prefetch=1,
            grid=(count,),
            in_specs=in_specs,
            out_specs=[pl.BlockSpec((hours_dev, unit), lambda i, place: (0, i)) for _ in peers],
        ),
        cost_estimate=pl.CostEstimate(
            flops=0,
            transcendentals=0,
            bytes_accessed=bytes_moved,
        ),
        name="pack",
    )(place, *operands)


def rows_kernel(place_ref, source, target):
    target[...] = source[...]


def order_rows(temporal_cov, place, groups):
    hours_all = temporal_cov.shape[0]
    hours_dev = hours_all // groups
    return pl.pallas_call(
        rows_kernel,
        out_shape=jax.ShapeDtypeStruct(temporal_cov.shape, temporal_cov.dtype),
        grid_spec=pltpu.PrefetchScalarGridSpec(
            num_scalar_prefetch=1,
            grid=(groups,),
            in_specs=[pl.BlockSpec((hours_dev, hours_all), lambda i, place: (place[i], 0))],
            out_specs=pl.BlockSpec((hours_dev, hours_all), lambda i, place: (i, 0)),
        ),
        name="order",
    )(place, temporal_cov)


def product_kernel(cfg, place_ref, neighbours_ref, counts_ref, cov_ref, *refs):
    groups, unit, block, slots, chunk_units, group_units, first_out, lead = cfg["dims"]
    opening, has_next = cfg["flags"]
    refs = list(refs)
    pieces = [refs.pop(0) for _ in range(groups)]
    inner = [refs.pop(0) for _ in range(groups)] if opening else None
    outset = [refs.pop(0) for _ in range(groups)] if opening else None
    carry_ref = None if opening else refs.pop(0)
    tiles_ref = refs.pop(0)
    outs = [refs.pop(0) for _ in range(groups)]
    next_ref = refs.pop(0) if has_next else None
    panel, mixed, banded = refs

    step = pl.program_id(0)
    steps = pl.num_programs(0)
    upward = ascends(place_ref[0])
    hours_dev = pieces[0].shape[0]
    reach = (slots - 1) // 2
    width = slots + 1

    def columns(position):
        at = jnp.where(upward, position, chunk_units + 1 - position)
        return pl.ds(pl.multiple_of(at * unit, unit), unit)

    @pl.when(step == 0)
    def _():
        for pair in range(banded.shape[0]):
            banded[pair, :block, slots * block :] = jnp.zeros((block, block), banded.dtype)
            banded[pair, block:, :block] = jnp.zeros((block, block), banded.dtype)
        if not opening:
            for which in range(2):
                mixed[:, columns(which)] = carry_ref[:, which * unit : (which + 1) * unit]

    def load(sources):
        for peer in range(groups):
            at = pl.multiple_of(place_ref[peer] * hours_dev, hours_dev)
            panel[pl.ds(at, hours_dev), :] = sources[peer][...]

    if opening:
        pl.when(step == 0)(lambda: load(inner))
        pl.when(step == 1)(lambda: load(outset))
        pl.when(step >= 2)(lambda: load(pieces))
    else:
        load(pieces)

    fresh = jnp.dot(cov_ref[...], panel[...], preferred_element_type=jnp.float32).astype(mixed.dtype)
    mixed[:, columns(step + lead)] = fresh
    if has_next:
        for which in range(2):

            @pl.when(step == steps - 2 + which)
            def _():
                next_ref[:, which * unit : (which + 1) * unit] = fresh

    @pl.when(step + lead >= 2)
    def _():
        turn = step + lead - 2
        at = jnp.where(upward, turn, chunk_units - 1 - turn)
        own_unit = jnp.where(upward, first_out + turn, group_units - 1 - first_out - turn)
        first_row = own_unit * (unit // block)
        base = pl.multiple_of(at * unit, unit)
        for pair in range(unit // block // 2):
            for which in range(2):
                row = 2 * pair + which
                mine = first_row + row
                block_id = place_ref[groups] + mine
                live = counts_ref[mine]
                for slot in range(slots):
                    offset = neighbours_ref[mine, slot] - block_id + (reach + which)
                    offset = jnp.clip(offset, 0, slots)
                    tile = tiles_ref[row, slot]
                    banded[
                        pair,
                        which * block : (which + 1) * block,
                        pl.ds(pl.multiple_of(offset * block, block), block),
                    ] = jnp.where(slot < live, tile, jnp.zeros_like(tile))
            window = mixed[:, pl.ds(pl.multiple_of(base + 2 * pair * block, block), width * block)]
            summed = lax.dot_general(
                window, banded[pair], (((1,), (1,)), ((), ())), preferred_element_type=jnp.float32
            ).astype(outs[0].dtype)
            for peer in range(groups):
                outs[peer][:, 2 * pair * block : 2 * (pair + 1) * block] = summed[
                    peer * hours_dev : (peer + 1) * hours_dev
                ]


def products(place, neighbours, counts, cov, pieces, start, carry, spatial_blocks, layout, chunk):
    groups, unit, block, slots, group_units, chunk_units = layout
    chunks = group_units // chunk_units
    hours_all, hours_dev = cov.shape[0], pieces[0].shape[0]
    opening, has_next = chunk == 0, chunk < chunks - 1
    lead = 0 if opening else 2
    steps = chunk_units + 2 - lead
    first_out = chunk * chunk_units

    def piece_index(i, place, *_):
        turn = jnp.maximum(i + lead - 2, 0)
        return 0, jnp.where(ascends(place[0]), turn, chunk_units - 1 - turn)

    def tile_index(i, place, *_):
        turn = first_out + jnp.maximum(i + lead - 2, 0)
        return jnp.where(ascends(place[0]), turn, group_units - 1 - turn), 0, 0, 0

    def whole(shape):
        return pl.BlockSpec(shape, lambda i, *_: (0, 0))

    piece_spec = pl.BlockSpec((hours_dev, unit), piece_index)
    in_specs = [whole((hours_all, hours_all))] + [piece_spec] * groups
    operands = [cov] + list(pieces)
    if opening:
        in_specs += [whole((hours_dev, unit))] * (2 * groups)
        operands += list(start[0]) + list(start[1])
    else:
        in_specs += [whole((hours_all, 2 * unit))]
        operands += [carry]
    blocks_unit = unit // block
    in_specs += [pl.BlockSpec((blocks_unit, slots, block, block), tile_index)]
    operands += [spatial_blocks]
    dtype = pieces[0].dtype
    out_shape = [jax.ShapeDtypeStruct((hours_dev, chunk_units * unit), dtype)] * groups
    out_specs = [piece_spec] * groups
    if has_next:
        out_shape += [jax.ShapeDtypeStruct((hours_all, 2 * unit), dtype)]
        out_specs += [whole((hours_all, 2 * unit))]
    cfg = {
        "dims": (groups, unit, block, slots, chunk_units, group_units, first_out, lead),
        "flags": (opening, has_next),
    }
    flops = 2 * hours_all * unit * (steps * hours_all + chunk_units * (slots + 1) * block)
    results = pl.pallas_call(
        functools.partial(product_kernel, cfg),
        out_shape=out_shape,
        grid_spec=pltpu.PrefetchScalarGridSpec(
            num_scalar_prefetch=3,
            grid=(steps,),
            in_specs=in_specs,
            out_specs=out_specs,
            scratch_shapes=[
                pltpu.VMEM((hours_all, unit), dtype),
                pltpu.VMEM((hours_all, (chunk_units + 2) * unit), dtype),
                pltpu.VMEM((blocks_unit // 2, 2 * block, (slots + 1) * block), dtype),
            ],
        ),
        compiler_params=pltpu.CompilerParams(vmem_limit_bytes=48 * MiB),
        cost_estimate=pl.CostEstimate(
            flops=flops,
            transcendentals=0,
            bytes_accessed=2 * hours_all * unit * (steps + chunk_units)
            + 2 * chunk_units * blocks_unit * slots * block * block,
        ),
        name="products",
    )(place, neighbours, counts, *operands)
    return results[:groups], (results[groups] if has_next else None)


def place_kernel(peers, chunks, chunk, place_ref, *refs):
    target, sems = refs[-2], refs[-1]
    copies = []
    for which, peer in enumerate(peers):
        source = refs[which]
        columns = source.shape[1]
        group = place_ref[peer]
        at = group * chunks + jnp.where(ascends(group), chunk, chunks - 1 - chunk)
        copies.append(
            pltpu.make_async_copy(
                source,
                target.at[:, pl.ds(pl.multiple_of(at * columns, columns), columns)],
                sems.at[which],
            )
        )
    for copy in copies:
        copy.start()
    for copy in copies:
        copy.wait()


def put(result, pieces, peers, place, cells_dev, chunks, chunk, on_chip):
    hours_dev, columns = pieces[0].shape
    in_specs = [pl.BlockSpec(memory_space=pltpu.VMEM)] * len(pieces)
    operands = list(pieces)
    if on_chip:
        operands = [pltpu.with_memory_space_constraint(piece, pltpu.VMEM) for piece in pieces]
    aliases = {}
    if result is not None:
        in_specs += [pl.BlockSpec(memory_space=pl.ANY)]
        operands += [result]
        aliases = {1 + len(pieces): 0}
    return pl.pallas_call(
        functools.partial(place_kernel, peers, chunks, chunk),
        out_shape=jax.ShapeDtypeStruct((hours_dev, cells_dev), pieces[0].dtype),
        grid_spec=pltpu.PrefetchScalarGridSpec(
            num_scalar_prefetch=1,
            grid=(),
            in_specs=in_specs,
            out_specs=pl.BlockSpec(memory_space=pl.ANY),
            scratch_shapes=[pltpu.SemaphoreType.DMA((len(pieces),))],
        ),
        input_output_aliases=aliases,
        cost_estimate=pl.CostEstimate(
            flops=0, transcendentals=0, bytes_accessed=4 * len(pieces) * hours_dev * columns
        ),
        name="place",
    )(place, *operands)


def per_device(field, temporal_cov, spatial_blocks, neighbours, counts):
    groups = lax.axis_size("tm")
    spaces = lax.axis_size("space")
    _, cells_dev = field.shape
    per_group, slots, block = spatial_blocks.shape[:3]
    reach = (slots - 1) // 2
    unit = reach * block
    group_units = per_group // reach
    chunk_units = CHUNK_UNITS if group_units % CHUNK_UNITS == 0 else group_units
    chunks = group_units // chunk_units
    layout = (groups, unit, block, slots, group_units, chunk_units)

    mine = lax.axis_index("tm")
    first_block = (lax.axis_index("space") * groups + mine) * per_group
    place = jnp.concatenate(
        [
            jnp.bitwise_xor(mine.astype(jnp.int32), jnp.arange(groups, dtype=jnp.int32)),
            first_block.astype(jnp.int32)[None],
        ]
    )

    def swap(array, peer):
        return lax.ppermute(array, "tm", [(at, at ^ peer) for at in range(groups)])

    def swap_all(arrays):
        moved = {peer: swap(arrays[peer], peer) for peer in range(groups - 1, 0, -1)}
        return [arrays[0]] + [moved[peer] for peer in range(1, groups)]

    forward = [(at, at + 1) for at in range(spaces - 1)]
    backward = [(to, at) for at, to in forward]
    peers = list(range(groups))

    first_sent = pack(field, place, None, peers, unit, group_units, 0, 1, groups, True)
    first = swap_all(first_sent)
    low = lax.ppermute(field[:, cells_dev - unit :], "space", forward)
    high = lax.ppermute(field[:, :unit], "space", backward)
    arrived, sent = [], first_sent
    for chunk in range(chunks):
        halo = (low, high) if chunk == chunks - 1 else None
        turn, _ = lax.optimization_barrier((place, sent[-1]))
        sent = pack(
            field, turn, halo, peers, unit, group_units,
            1 + chunk * chunk_units, chunk_units, groups,
        )
        arrived.append(swap_all(sent))
    inner = [first_sent[1]] + [swap(first[peer ^ 1], 1) for peer in range(1, groups)]
    cov = order_rows(temporal_cov, place, groups)
    carry, result = None, None
    returned = []
    for chunk in range(chunks):
        outs, carry = products(
            place, neighbours, counts, cov, arrived[chunk], (inner, first), carry,
            spatial_blocks, layout, chunk,
        )
        returned.append(swap_all(outs))
    for chunk in range(chunks):
        closing = chunk == chunks - 1
        parts = [peers[:2], peers[:2:-1], peers[2:3]] if closing else [peers]
        for part, listed in enumerate(parts):
            if listed:
                result = put(
                    result, [returned[chunk][peer] for peer in listed], listed, place,
                    cells_dev, chunks, chunk, closing and part > 0,
                )
    return result


def solution(mesh):
    placed = (
        P("tm", "space"),
        P(),
        P(("space", "tm"), None, None, None),
        P(("space", "tm"), None),
        P(("space", "tm")),
    )
    return jax.shard_map(
        per_device, mesh=mesh, in_specs=placed, out_specs=P("tm", "space"), check_vma=False
    )
```

```python
import functools

import jax
import jax.numpy as jnp
from jax import lax
from jax.experimental import pallas as pl
from jax.experimental.pallas import tpu as pltpu
from jax.sharding import PartitionSpec as P


CHUNK_UNITS = 6
ROW_COPIES = 4
MiB = 1 << 20


def ascends(group):
    return jnp.bitwise_and(group, 1) == 1


def pack_kernel(last, sources, place_ref, *refs):
    inputs, targets = refs[: -len(sources)], refs[-len(sources) :]
    low_ref, high_ref = inputs[len(sources) :]
    for peer, target in enumerate(targets):
        at = sources[peer](pl.program_id(0), place_ref)
        target[...] = jnp.where(
            at < 0, low_ref[...], jnp.where(at > last, high_ref[...], inputs[peer][...])
        )


def copy_kernel(unit, sources, peers, on_chip, *refs):
    if on_chip:
        mine = lax.axis_index("tm")
        place_ref = {peer: jnp.bitwise_xor(mine, peer) for peer in peers}
        field_ref, *refs = refs
    else:
        place_ref, field_ref, *refs = refs
    count = len(sources)
    targets, sems = refs[:count], refs[-1]
    gathered = targets if on_chip else [refs[count].at[which] for which in range(count)]
    columns = targets[0].shape[1]
    reads, writes = [], []
    for which, source in enumerate(sources):
        at = pl.multiple_of(source(0, place_ref) * unit, unit)
        reads.append(
            pltpu.make_async_copy(
                field_ref.at[:, pl.ds(at, columns)], gathered[which], sems.at[0, which]
            )
        )
        if not on_chip:
            writes.append(
                pltpu.make_async_copy(gathered[which], targets[which], sems.at[1, which])
            )
    for read in reads:
        read.start()
    for which, read in enumerate(reads):
        read.wait()
        if writes:
            writes[which].start()
    for write in writes:
        write.wait()


def pack(field, place, halo, peers, unit, group_units, first, count, groups, on_chip=False):
    hours_dev = field.shape[0]
    last = groups * group_units - 1

    def source_of(peer):
        def source(i, place):
            group = place[peer]
            start = jnp.where(ascends(group), first, group_units - first - count)
            return group * group_units + start + i

        return source

    sources = [source_of(peer) for peer in peers]

    def spec(source):
        return pl.BlockSpec(
            (hours_dev, unit), lambda i, place: (0, jnp.clip(source(i, place), 0, last))
        )

    bytes_moved = 4 * len(peers) * hours_dev * count * unit
    if halo is None:
        shape = (hours_dev, count * unit)
        kind = pltpu.VMEM if on_chip else jax.ShapeDtypeStruct
        space = pltpu.VMEM if on_chip else pl.ANY
        scratch = [] if on_chip else [pltpu.VMEM((len(peers),) + shape, field.dtype)]
        operands = [field] if on_chip else [place, field]
        return pl.pallas_call(
            functools.partial(copy_kernel, unit, sources, peers, on_chip),
            out_shape=[kind(shape, field.dtype) for _ in peers],
            grid_spec=pltpu.PrefetchScalarGridSpec(
                num_scalar_prefetch=len(operands) - 1,
                grid=(),
                in_specs=[pl.BlockSpec(memory_space=pl.ANY)],
                out_specs=[pl.BlockSpec(memory_space=space) for _ in peers],
                scratch_shapes=scratch + [pltpu.SemaphoreType.DMA((2, len(peers)))],
            ),
            cost_estimate=pl.CostEstimate(
                flops=0, transcendentals=0, bytes_accessed=bytes_moved
            ),
            name="pack",
        )(*operands)
    in_specs = [spec(source) for source in sources]
    operands = [field] * len(peers)
    in_specs += [pl.BlockSpec((hours_dev, unit), lambda i, place: (0, 0))] * 2
    operands += list(halo)
    return pl.pallas_call(
        functools.partial(pack_kernel, last, sources),
        out_shape=[jax.ShapeDtypeStruct((hours_dev, count * unit), field.dtype) for _ in peers],
        grid_spec=pltpu.PrefetchScalarGridSpec(
            num_scalar_prefetch=1,
            grid=(count,),
            in_specs=in_specs,
            out_specs=[pl.BlockSpec((hours_dev, unit), lambda i, place: (0, i)) for _ in peers],
        ),
        cost_estimate=pl.CostEstimate(
            flops=0,
            transcendentals=0,
            bytes_accessed=bytes_moved,
        ),
        name="pack",
    )(place, *operands)


def rows_kernel(place_ref, source, target):
    target[...] = source[...]


def order_rows(temporal_cov, place, groups):
    hours_all = temporal_cov.shape[0]
    hours_dev = hours_all // groups
    return pl.pallas_call(
        rows_kernel,
        out_shape=jax.ShapeDtypeStruct(temporal_cov.shape, temporal_cov.dtype),
        grid_spec=pltpu.PrefetchScalarGridSpec(
            num_scalar_prefetch=1,
            grid=(groups,),
            in_specs=[pl.BlockSpec((hours_dev, hours_all), lambda i, place: (place[i], 0))],
            out_specs=pl.BlockSpec((hours_dev, hours_all), lambda i, place: (i, 0)),
        ),
        name="order",
    )(place, temporal_cov)


def product_kernel(cfg, place_ref, neighbours_ref, counts_ref, cov_ref, *refs):
    groups, unit, block, slots, chunk_units, group_units, first_out, lead = cfg["dims"]
    opening, has_next = cfg["flags"]
    refs = list(refs)
    pieces = [refs.pop(0) for _ in range(groups)]
    inner = [refs.pop(0) for _ in range(groups)] if opening else None
    outset = [refs.pop(0) for _ in range(groups)] if opening else None
    carry_ref = None if opening else refs.pop(0)
    tiles_ref = refs.pop(0)
    outs = [refs.pop(0) for _ in range(groups)]
    next_ref = refs.pop(0) if has_next else None
    panel, mixed, banded = refs

    step = pl.program_id(0)
    steps = pl.num_programs(0)
    upward = ascends(place_ref[0])
    hours_dev = pieces[0].shape[0]
    reach = (slots - 1) // 2
    width = slots + 1

    def columns(position):
        at = jnp.where(upward, position, chunk_units + 1 - position)
        return pl.ds(pl.multiple_of(at * unit, unit), unit)

    @pl.when(step == 0)
    def _():
        for pair in range(banded.shape[0]):
            banded[pair, :block, slots * block :] = jnp.zeros((block, block), banded.dtype)
            banded[pair, block:, :block] = jnp.zeros((block, block), banded.dtype)
        if not opening:
            for which in range(2):
                mixed[:, columns(which)] = carry_ref[:, which * unit : (which + 1) * unit]

    def load(sources):
        for peer in range(groups):
            at = pl.multiple_of(place_ref[peer] * hours_dev, hours_dev)
            panel[pl.ds(at, hours_dev), :] = sources[peer][...]

    if opening:
        pl.when(step == 0)(lambda: load(inner))
        pl.when(step == 1)(lambda: load(outset))
        pl.when(step >= 2)(lambda: load(pieces))
    else:
        load(pieces)

    fresh = jnp.dot(cov_ref[...], panel[...], preferred_element_type=jnp.float32).astype(mixed.dtype)
    mixed[:, columns(step + lead)] = fresh
    if has_next:
        for which in range(2):

            @pl.when(step == steps - 2 + which)
            def _():
                next_ref[:, which * unit : (which + 1) * unit] = fresh

    @pl.when(step + lead >= 2)
    def _():
        turn = step + lead - 2
        at = jnp.where(upward, turn, chunk_units - 1 - turn)
        own_unit = jnp.where(upward, first_out + turn, group_units - 1 - first_out - turn)
        first_row = own_unit * (unit // block)
        base = pl.multiple_of(at * unit, unit)
        for pair in range(unit // block // 2):
            for which in range(2):
                row = 2 * pair + which
                mine = first_row + row
                block_id = place_ref[groups] + mine
                live = counts_ref[mine]
                for slot in range(slots):
                    offset = neighbours_ref[mine, slot] - block_id + (reach + which)
                    offset = jnp.clip(offset, 0, slots)
                    tile = tiles_ref[row, slot]
                    banded[
                        pair,
                        which * block : (which + 1) * block,
                        pl.ds(pl.multiple_of(offset * block, block), block),
                    ] = jnp.where(slot < live, tile, jnp.zeros_like(tile))
            window = mixed[:, pl.ds(pl.multiple_of(base + 2 * pair * block, block), width * block)]
            summed = lax.dot_general(
                window, banded[pair], (((1,), (1,)), ((), ())), preferred_element_type=jnp.float32
            ).astype(outs[0].dtype)
            for peer in range(groups):
                outs[peer][:, 2 * pair * block : 2 * (pair + 1) * block] = summed[
                    peer * hours_dev : (peer + 1) * hours_dev
                ]


def products(place, neighbours, counts, cov, pieces, start, carry, spatial_blocks, layout, chunk):
    groups, unit, block, slots, group_units, chunk_units = layout
    chunks = group_units // chunk_units
    hours_all, hours_dev = cov.shape[0], pieces[0].shape[0]
    opening, has_next = chunk == 0, chunk < chunks - 1
    lead = 0 if opening else 2
    steps = chunk_units + 2 - lead
    first_out = chunk * chunk_units

    def piece_index(i, place, *_):
        turn = jnp.maximum(i + lead - 2, 0)
        return 0, jnp.where(ascends(place[0]), turn, chunk_units - 1 - turn)

    def tile_index(i, place, *_):
        turn = first_out + jnp.maximum(i + lead - 2, 0)
        return jnp.where(ascends(place[0]), turn, group_units - 1 - turn), 0, 0, 0

    def whole(shape):
        return pl.BlockSpec(shape, lambda i, *_: (0, 0))

    piece_spec = pl.BlockSpec((hours_dev, unit), piece_index)
    in_specs = [whole((hours_all, hours_all))] + [piece_spec] * groups
    operands = [cov] + list(pieces)
    if opening:
        in_specs += [whole((hours_dev, unit))] * (2 * groups)
        operands += list(start[0]) + list(start[1])
    else:
        in_specs += [whole((hours_all, 2 * unit))]
        operands += [carry]
    blocks_unit = unit // block
    in_specs += [pl.BlockSpec((blocks_unit, slots, block, block), tile_index)]
    operands += [spatial_blocks]
    dtype = pieces[0].dtype
    out_shape = [jax.ShapeDtypeStruct((hours_dev, chunk_units * unit), dtype)] * groups
    out_specs = [piece_spec] * groups
    if has_next:
        out_shape += [jax.ShapeDtypeStruct((hours_all, 2 * unit), dtype)]
        out_specs += [whole((hours_all, 2 * unit))]
    cfg = {
        "dims": (groups, unit, block, slots, chunk_units, group_units, first_out, lead),
        "flags": (opening, has_next),
    }
    flops = 2 * hours_all * unit * (steps * hours_all + chunk_units * (slots + 1) * block)
    results = pl.pallas_call(
        functools.partial(product_kernel, cfg),
        out_shape=out_shape,
        grid_spec=pltpu.PrefetchScalarGridSpec(
            num_scalar_prefetch=3,
            grid=(steps,),
            in_specs=in_specs,
            out_specs=out_specs,
            scratch_shapes=[
                pltpu.VMEM((hours_all, unit), dtype),
                pltpu.VMEM((hours_all, (chunk_units + 2) * unit), dtype),
                pltpu.VMEM((blocks_unit // 2, 2 * block, (slots + 1) * block), dtype),
            ],
        ),
        compiler_params=pltpu.CompilerParams(vmem_limit_bytes=48 * MiB),
        cost_estimate=pl.CostEstimate(
            flops=flops,
            transcendentals=0,
            bytes_accessed=2 * hours_all * unit * (steps + chunk_units)
            + 2 * chunk_units * blocks_unit * slots * block * block,
        ),
        name="products",
    )(place, neighbours, counts, *operands)
    return results[:groups], (results[groups] if has_next else None)


def place_kernel(peers, chunks, chunk, place_ref, *refs):
    target, sems = refs[-2], refs[-1]
    copies = []
    for which, peer in enumerate(peers):
        source = refs[which]
        columns = source.shape[1]
        group = place_ref[peer]
        at = group * chunks + jnp.where(ascends(group), chunk, chunks - 1 - chunk)
        rows = source.shape[0] // ROW_COPIES
        for part in range(ROW_COPIES):
            copies.append(
                pltpu.make_async_copy(
                    source.at[part * rows : (part + 1) * rows],
                    target.at[
                        part * rows : (part + 1) * rows,
                        pl.ds(pl.multiple_of(at * columns, columns), columns),
                    ],
                    sems.at[which, part],
                )
            )
    for copy in copies:
        copy.start()
    for copy in copies:
        copy.wait()


def put(result, pieces, peers, place, cells_dev, chunks, chunk, on_chip):
    hours_dev, columns = pieces[0].shape
    in_specs = [pl.BlockSpec(memory_space=pltpu.VMEM)] * len(pieces)
    operands = list(pieces)
    if on_chip:
        operands = [pltpu.with_memory_space_constraint(piece, pltpu.VMEM) for piece in pieces]
    aliases = {}
    if result is not None:
        in_specs += [pl.BlockSpec(memory_space=pl.ANY)]
        operands += [result]
        aliases = {1 + len(pieces): 0}
    return pl.pallas_call(
        functools.partial(place_kernel, peers, chunks, chunk),
        out_shape=jax.ShapeDtypeStruct((hours_dev, cells_dev), pieces[0].dtype),
        grid_spec=pltpu.PrefetchScalarGridSpec(
            num_scalar_prefetch=1,
            grid=(),
            in_specs=in_specs,
            out_specs=pl.BlockSpec(memory_space=pl.ANY),
            scratch_shapes=[pltpu.SemaphoreType.DMA((len(pieces), ROW_COPIES))],
        ),
        input_output_aliases=aliases,
        cost_estimate=pl.CostEstimate(
            flops=0, transcendentals=0, bytes_accessed=4 * len(pieces) * hours_dev * columns
        ),
        name="place",
    )(place, *operands)


def per_device(field, temporal_cov, spatial_blocks, neighbours, counts):
    groups = lax.axis_size("tm")
    spaces = lax.axis_size("space")
    _, cells_dev = field.shape
    per_group, slots, block = spatial_blocks.shape[:3]
    reach = (slots - 1) // 2
    unit = reach * block
    group_units = per_group // reach
    chunk_units = CHUNK_UNITS if group_units % CHUNK_UNITS == 0 else group_units
    chunks = group_units // chunk_units
    layout = (groups, unit, block, slots, group_units, chunk_units)

    mine = lax.axis_index("tm")
    first_block = (lax.axis_index("space") * groups + mine) * per_group
    place = jnp.concatenate(
        [
            jnp.bitwise_xor(mine.astype(jnp.int32), jnp.arange(groups, dtype=jnp.int32)),
            first_block.astype(jnp.int32)[None],
        ]
    )

    peers = list(range(groups))

    def swap(array, peer):
        return lax.ppermute(array, "tm", [(at, at ^ peer) for at in range(groups)])

    def swap_all(arrays):
        moved = {peer: swap(arrays[peer], peer) for peer in peers[2:] + peers[1:2]}
        return [arrays[0]] + [moved[peer] for peer in range(1, groups)]

    forward = [(at, at + 1) for at in range(spaces - 1)]
    backward = [(to, at) for at, to in forward]

    far = pack(field, None, None, peers[2:], unit, group_units, 0, 1, groups, True)
    near = pack(field, None, None, peers[:2], unit, group_units, 0, 1, groups, True)
    first_sent = near + far
    first = swap_all(first_sent)
    low = lax.ppermute(field[:, cells_dev - unit :], "space", forward)
    high = lax.ppermute(field[:, :unit], "space", backward)
    arrived, sent = [], first_sent
    for chunk in range(chunks):
        halo = (low, high) if chunk == chunks - 1 else None
        turn, _ = lax.optimization_barrier((place, sent[-1]))
        sent = pack(
            field, turn, halo, peers, unit, group_units,
            1 + chunk * chunk_units, chunk_units, groups,
        )
        arrived.append(swap_all(sent))
    inner = [first_sent[1]] + [swap(first[peer ^ 1], 1) for peer in range(1, groups)]
    cov = order_rows(temporal_cov, place, groups)
    carry, result = None, None
    returned = []
    for chunk in range(chunks):
        outs, carry = products(
            place, neighbours, counts, cov, arrived[chunk], (inner, first), carry,
            spatial_blocks, layout, chunk,
        )
        returned.append(swap_all(outs))
    for chunk in range(chunks):
        closing = chunk == chunks - 1
        parts = [peers[:2], peers[2:-1], peers[-1:]] if closing else [peers]
        for part, listed in enumerate(parts):
            if listed:
                result = put(
                    result, [returned[chunk][peer] for peer in listed], listed, place,
                    cells_dev, chunks, chunk, closing and part > 0,
                )
    return result


def solution(mesh):
    placed = (
        P("tm", "space"),
        P(),
        P(("space", "tm"), None, None, None),
        P(("space", "tm"), None),
        P(("space", "tm")),
    )
    return jax.shard_map(
        per_device, mesh=mesh, in_specs=placed, out_specs=P("tm", "space"), check_vma=False
    )
```

```python
import functools

import jax
import jax.numpy as jnp
from jax import lax
from jax.experimental import pallas as pl
from jax.experimental.pallas import tpu as pltpu
from jax.sharding import PartitionSpec as P


CHUNK_UNITS = 6
ROW_COPIES = 4
MiB = 1 << 20


def ascends(group):
    return jnp.bitwise_and(group, 1) == 1


def pack_kernel(last, sources, place_ref, *refs):
    inputs, targets = refs[: -len(sources)], refs[-len(sources) :]
    low_ref, high_ref = inputs[len(sources) :]
    for peer, target in enumerate(targets):
        at = sources[peer](pl.program_id(0), place_ref)
        target[...] = jnp.where(
            at < 0, low_ref[...], jnp.where(at > last, high_ref[...], inputs[peer][...])
        )


def copy_kernel(unit, sources, peers, on_chip, *refs):
    if on_chip:
        mine = lax.axis_index("tm")
        place_ref = {peer: jnp.bitwise_xor(mine, peer) for peer in peers}
        field_ref, *refs = refs
    else:
        place_ref, field_ref, *refs = refs
    count = len(sources)
    targets, sems = refs[:count], refs[-1]
    gathered = targets if on_chip else [refs[count].at[which] for which in range(count)]
    columns = targets[0].shape[1]
    reads, writes = [], []
    for which, source in enumerate(sources):
        at = pl.multiple_of(source(0, place_ref) * unit, unit)
        reads.append(
            pltpu.make_async_copy(
                field_ref.at[:, pl.ds(at, columns)], gathered[which], sems.at[0, which]
            )
        )
        if not on_chip:
            writes.append(
                pltpu.make_async_copy(gathered[which], targets[which], sems.at[1, which])
            )
    for read in reads:
        read.start()
    for which, read in enumerate(reads):
        read.wait()
        if writes:
            writes[which].start()
    for write in writes:
        write.wait()


def pack(field, place, halo, peers, unit, group_units, first, count, groups, on_chip=False):
    hours_dev = field.shape[0]
    last = groups * group_units - 1

    def source_of(peer):
        def source(i, place):
            group = place[peer]
            start = jnp.where(ascends(group), first, group_units - first - count)
            return group * group_units + start + i

        return source

    sources = [source_of(peer) for peer in peers]

    def spec(source):
        return pl.BlockSpec(
            (hours_dev, unit), lambda i, place: (0, jnp.clip(source(i, place), 0, last))
        )

    bytes_moved = 4 * len(peers) * hours_dev * count * unit
    if halo is None:
        shape = (hours_dev, count * unit)
        kind = pltpu.VMEM if on_chip else jax.ShapeDtypeStruct
        space = pltpu.VMEM if on_chip else pl.ANY
        scratch = [] if on_chip else [pltpu.VMEM((len(peers),) + shape, field.dtype)]
        operands = [field] if on_chip else [place, field]
        return pl.pallas_call(
            functools.partial(copy_kernel, unit, sources, peers, on_chip),
            out_shape=[kind(shape, field.dtype) for _ in peers],
            grid_spec=pltpu.PrefetchScalarGridSpec(
                num_scalar_prefetch=len(operands) - 1,
                grid=(),
                in_specs=[pl.BlockSpec(memory_space=pl.ANY)],
                out_specs=[pl.BlockSpec(memory_space=space) for _ in peers],
                scratch_shapes=scratch + [pltpu.SemaphoreType.DMA((2, len(peers)))],
            ),
            cost_estimate=pl.CostEstimate(
                flops=0, transcendentals=0, bytes_accessed=bytes_moved
            ),
            name="pack",
        )(*operands)
    in_specs = [spec(source) for source in sources]
    operands = [field] * len(peers)
    in_specs += [pl.BlockSpec((hours_dev, unit), lambda i, place: (0, 0))] * 2
    operands += list(halo)
    return pl.pallas_call(
        functools.partial(pack_kernel, last, sources),
        out_shape=[jax.ShapeDtypeStruct((hours_dev, count * unit), field.dtype) for _ in peers],
        grid_spec=pltpu.PrefetchScalarGridSpec(
            num_scalar_prefetch=1,
            grid=(count,),
            in_specs=in_specs,
            out_specs=[pl.BlockSpec((hours_dev, unit), lambda i, place: (0, i)) for _ in peers],
        ),
        cost_estimate=pl.CostEstimate(
            flops=0,
            transcendentals=0,
            bytes_accessed=bytes_moved,
        ),
        name="pack",
    )(place, *operands)


def rows_kernel(place_ref, source, target):
    target[...] = source[...]


def order_rows(temporal_cov, place, groups):
    hours_all = temporal_cov.shape[0]
    hours_dev = hours_all // groups
    return pl.pallas_call(
        rows_kernel,
        out_shape=jax.ShapeDtypeStruct(temporal_cov.shape, temporal_cov.dtype),
        grid_spec=pltpu.PrefetchScalarGridSpec(
            num_scalar_prefetch=1,
            grid=(groups,),
            in_specs=[pl.BlockSpec((hours_dev, hours_all), lambda i, place: (place[i], 0))],
            out_specs=pl.BlockSpec((hours_dev, hours_all), lambda i, place: (i, 0)),
        ),
        name="order",
    )(place, temporal_cov)


def product_kernel(cfg, place_ref, neighbours_ref, counts_ref, cov_ref, *refs):
    groups, unit, block, slots, chunk_units, group_units, first_out, lead = cfg["dims"]
    opening, has_next = cfg["flags"]
    refs = list(refs)
    pieces = [refs.pop(0) for _ in range(groups)]
    inner = [refs.pop(0) for _ in range(groups)] if opening else None
    outset = [refs.pop(0) for _ in range(groups)] if opening else None
    carry_ref = None if opening else refs.pop(0)
    tiles_ref = refs.pop(0)
    outs = [refs.pop(0) for _ in range(groups)]
    next_ref = refs.pop(0) if has_next else None
    panel, mixed, banded = refs

    step = pl.program_id(0)
    steps = pl.num_programs(0)
    upward = ascends(place_ref[0])
    hours_dev = pieces[0].shape[0]
    reach = (slots - 1) // 2
    width = slots + 1

    def columns(position):
        at = jnp.where(upward, position, chunk_units + 1 - position)
        return pl.ds(pl.multiple_of(at * unit, unit), unit)

    @pl.when(step == 0)
    def _():
        for pair in range(banded.shape[0]):
            banded[pair, :block, slots * block :] = jnp.zeros((block, block), banded.dtype)
            banded[pair, block:, :block] = jnp.zeros((block, block), banded.dtype)
        if not opening:
            for which in range(2):
                mixed[:, columns(which)] = carry_ref[:, which * unit : (which + 1) * unit]

    def load(sources):
        for peer in range(groups):
            at = pl.multiple_of(place_ref[peer] * hours_dev, hours_dev)
            panel[pl.ds(at, hours_dev), :] = sources[peer][...]

    if opening:
        pl.when(step == 0)(lambda: load(inner))
        pl.when(step == 1)(lambda: load(outset))
        pl.when(step >= 2)(lambda: load(pieces))
    else:
        load(pieces)

    fresh = jnp.dot(cov_ref[...], panel[...], preferred_element_type=jnp.float32).astype(mixed.dtype)
    mixed[:, columns(step + lead)] = fresh
    if has_next:
        for which in range(2):

            @pl.when(step == steps - 2 + which)
            def _():
                next_ref[:, which * unit : (which + 1) * unit] = fresh

    @pl.when(step + lead >= 2)
    def _():
        turn = step + lead - 2
        at = jnp.where(upward, turn, chunk_units - 1 - turn)
        own_unit = jnp.where(upward, first_out + turn, group_units - 1 - first_out - turn)
        first_row = own_unit * (unit // block)
        base = pl.multiple_of(at * unit, unit)
        for pair in range(unit // block // 2):
            for which in range(2):
                row = 2 * pair + which
                mine = first_row + row
                block_id = place_ref[groups] + mine
                live = counts_ref[mine]
                for slot in range(slots):
                    offset = neighbours_ref[mine, slot] - block_id + (reach + which)
                    offset = jnp.clip(offset, 0, slots)
                    tile = tiles_ref[row, slot]
                    banded[
                        pair,
                        which * block : (which + 1) * block,
                        pl.ds(pl.multiple_of(offset * block, block), block),
                    ] = jnp.where(slot < live, tile, jnp.zeros_like(tile))
            window = mixed[:, pl.ds(pl.multiple_of(base + 2 * pair * block, block), width * block)]
            summed = lax.dot_general(
                window, banded[pair], (((1,), (1,)), ((), ())), preferred_element_type=jnp.float32
            ).astype(outs[0].dtype)
            for peer in range(groups):
                outs[peer][:, 2 * pair * block : 2 * (pair + 1) * block] = summed[
                    peer * hours_dev : (peer + 1) * hours_dev
                ]


def products(place, neighbours, counts, cov, pieces, start, carry, spatial_blocks, layout, chunk):
    groups, unit, block, slots, group_units, chunk_units = layout
    chunks = group_units // chunk_units
    hours_all, hours_dev = cov.shape[0], pieces[0].shape[0]
    opening, has_next = chunk == 0, chunk < chunks - 1
    lead = 0 if opening else 2
    steps = chunk_units + 2 - lead
    first_out = chunk * chunk_units

    def piece_index(i, place, *_):
        turn = jnp.maximum(i + lead - 2, 0)
        return 0, jnp.where(ascends(place[0]), turn, chunk_units - 1 - turn)

    def tile_index(i, place, *_):
        turn = first_out + jnp.maximum(i + lead - 2, 0)
        return jnp.where(ascends(place[0]), turn, group_units - 1 - turn), 0, 0, 0

    def whole(shape):
        return pl.BlockSpec(shape, lambda i, *_: (0, 0))

    piece_spec = pl.BlockSpec((hours_dev, unit), piece_index)
    in_specs = [whole((hours_all, hours_all))] + [piece_spec] * groups
    operands = [cov] + list(pieces)
    if opening:
        in_specs += [whole((hours_dev, unit))] * (2 * groups)
        operands += list(start[0]) + list(start[1])
    else:
        in_specs += [whole((hours_all, 2 * unit))]
        operands += [carry]
    blocks_unit = unit // block
    in_specs += [pl.BlockSpec((blocks_unit, slots, block, block), tile_index)]
    operands += [spatial_blocks]
    dtype = pieces[0].dtype
    out_shape = [jax.ShapeDtypeStruct((hours_dev, chunk_units * unit), dtype)] * groups
    out_specs = [piece_spec] * groups
    if has_next:
        out_shape += [jax.ShapeDtypeStruct((hours_all, 2 * unit), dtype)]
        out_specs += [whole((hours_all, 2 * unit))]
    cfg = {
        "dims": (groups, unit, block, slots, chunk_units, group_units, first_out, lead),
        "flags": (opening, has_next),
    }
    flops = 2 * hours_all * unit * (steps * hours_all + chunk_units * (slots + 1) * block)
    results = pl.pallas_call(
        functools.partial(product_kernel, cfg),
        out_shape=out_shape,
        grid_spec=pltpu.PrefetchScalarGridSpec(
            num_scalar_prefetch=3,
            grid=(steps,),
            in_specs=in_specs,
            out_specs=out_specs,
            scratch_shapes=[
                pltpu.VMEM((hours_all, unit), dtype),
                pltpu.VMEM((hours_all, (chunk_units + 2) * unit), dtype),
                pltpu.VMEM((blocks_unit // 2, 2 * block, (slots + 1) * block), dtype),
            ],
        ),
        compiler_params=pltpu.CompilerParams(vmem_limit_bytes=48 * MiB),
        cost_estimate=pl.CostEstimate(
            flops=flops,
            transcendentals=0,
            bytes_accessed=2 * hours_all * unit * (steps + chunk_units)
            + 2 * chunk_units * blocks_unit * slots * block * block,
        ),
        name="products",
    )(place, neighbours, counts, *operands)
    return results[:groups], (results[groups] if has_next else None)


def place_kernel(peers, chunks, chunk, on_chip, *refs):
    target, sems = refs[-2], refs[-1]
    if on_chip:
        mine = lax.axis_index("tm")
        place_ref = {peer: jnp.bitwise_xor(mine, peer) for peer in peers}
    else:
        place_ref, *refs = refs
    copies = []
    for which, peer in enumerate(peers):
        source = refs[which]
        columns = source.shape[1]
        group = place_ref[peer]
        at = group * chunks + jnp.where(ascends(group), chunk, chunks - 1 - chunk)
        rows = source.shape[0] // ROW_COPIES
        for part in range(ROW_COPIES):
            copies.append(
                pltpu.make_async_copy(
                    source.at[part * rows : (part + 1) * rows],
                    target.at[
                        part * rows : (part + 1) * rows,
                        pl.ds(pl.multiple_of(at * columns, columns), columns),
                    ],
                    sems.at[which, part],
                )
            )
    for copy in copies:
        copy.start()
    for copy in copies:
        copy.wait()


def put(result, pieces, peers, place, cells_dev, chunks, chunk, on_chip):
    hours_dev, columns = pieces[0].shape
    in_specs = [pl.BlockSpec(memory_space=pltpu.VMEM)] * len(pieces)
    operands = list(pieces)
    scalars = [] if on_chip else [place]
    if on_chip:
        operands = [pltpu.with_memory_space_constraint(piece, pltpu.VMEM) for piece in pieces]
    aliases = {}
    if result is not None:
        in_specs += [pl.BlockSpec(memory_space=pl.ANY)]
        operands += [result]
        aliases = {len(scalars) + len(pieces): 0}
    return pl.pallas_call(
        functools.partial(place_kernel, peers, chunks, chunk, on_chip),
        out_shape=jax.ShapeDtypeStruct((hours_dev, cells_dev), pieces[0].dtype),
        grid_spec=pltpu.PrefetchScalarGridSpec(
            num_scalar_prefetch=len(scalars),
            grid=(),
            in_specs=in_specs,
            out_specs=pl.BlockSpec(memory_space=pl.ANY),
            scratch_shapes=[pltpu.SemaphoreType.DMA((len(pieces), ROW_COPIES))],
        ),
        input_output_aliases=aliases,
        cost_estimate=pl.CostEstimate(
            flops=0, transcendentals=0, bytes_accessed=4 * len(pieces) * hours_dev * columns
        ),
        name="place",
    )(*scalars, *operands)


def per_device(field, temporal_cov, spatial_blocks, neighbours, counts):
    groups = lax.axis_size("tm")
    spaces = lax.axis_size("space")
    _, cells_dev = field.shape
    per_group, slots, block = spatial_blocks.shape[:3]
    reach = (slots - 1) // 2
    unit = reach * block
    group_units = per_group // reach
    chunk_units = CHUNK_UNITS if group_units % CHUNK_UNITS == 0 else group_units
    chunks = group_units // chunk_units
    layout = (groups, unit, block, slots, group_units, chunk_units)

    mine = lax.axis_index("tm")
    first_block = (lax.axis_index("space") * groups + mine) * per_group
    place = jnp.concatenate(
        [
            jnp.bitwise_xor(mine.astype(jnp.int32), jnp.arange(groups, dtype=jnp.int32)),
            first_block.astype(jnp.int32)[None],
        ]
    )

    peers = list(range(groups))

    def swap(array, peer):
        return lax.ppermute(array, "tm", [(at, at ^ peer) for at in range(groups)])

    def swap_all(arrays):
        moved = {peer: swap(arrays[peer], peer) for peer in peers[2:] + peers[1:2]}
        return [arrays[0]] + [moved[peer] for peer in range(1, groups)]

    forward = [(at, at + 1) for at in range(spaces - 1)]
    backward = [(to, at) for at, to in forward]

    far = pack(field, None, None, peers[2:], unit, group_units, 0, 1, groups, True)
    near = pack(field, None, None, peers[:2], unit, group_units, 0, 1, groups, True)
    first_sent = near + far
    first = swap_all(first_sent)
    low = lax.ppermute(field[:, cells_dev - unit :], "space", forward)
    high = lax.ppermute(field[:, :unit], "space", backward)
    arrived, sent = [], first_sent
    for chunk in range(chunks):
        halo = (low, high) if chunk == chunks - 1 else None
        turn, _ = lax.optimization_barrier((place, sent[-1]))
        sent = pack(
            field, turn, halo, peers, unit, group_units,
            1 + chunk * chunk_units, chunk_units, groups,
        )
        arrived.append(swap_all(sent))
    inner = [first_sent[1]] + [swap(first[peer ^ 1], 1) for peer in range(1, groups)]
    cov = order_rows(temporal_cov, place, groups)
    carry, result = None, None
    returned = []
    for chunk in range(chunks):
        outs, carry = products(
            place, neighbours, counts, cov, arrived[chunk], (inner, first), carry,
            spatial_blocks, layout, chunk,
        )
        returned.append(swap_all(outs))
    for chunk in range(chunks):
        closing = chunk == chunks - 1
        parts = [peers[:2], peers[2:-1], peers[-1:]] if closing else [peers]
        for part, listed in enumerate(parts):
            if listed:
                result = put(
                    result, [returned[chunk][peer] for peer in listed], listed, place,
                    cells_dev, chunks, chunk, closing and part > 0,
                )
    return result


def solution(mesh):
    placed = (
        P("tm", "space"),
        P(),
        P(("space", "tm"), None, None, None),
        P(("space", "tm"), None),
        P(("space", "tm")),
    )
    return jax.shard_map(
        per_device, mesh=mesh, in_specs=placed, out_specs=P("tm", "space"), check_vma=False
    )
```

```python
import functools

import jax
import jax.numpy as jnp
from jax import lax
from jax.experimental import pallas as pl
from jax.experimental.pallas import tpu as pltpu
from jax.sharding import PartitionSpec as P


CHUNK_UNITS = 6
ROW_COPIES = 4
MiB = 1 << 20


def ascends(group):
    return jnp.bitwise_and(group, 1) == 1


def pack_kernel(last, sources, place_ref, *refs):
    inputs, targets = refs[: -len(sources)], refs[-len(sources) :]
    low_ref, high_ref = inputs[len(sources) :]
    for peer, target in enumerate(targets):
        at = sources[peer](pl.program_id(0), place_ref)
        target[...] = jnp.where(
            at < 0, low_ref[...], jnp.where(at > last, high_ref[...], inputs[peer][...])
        )


def copy_kernel(unit, sources, peers, on_chip, *refs):
    if on_chip:
        mine = lax.axis_index("tm")
        place_ref = {peer: jnp.bitwise_xor(mine, peer) for peer in peers}
        field_ref, *refs = refs
    else:
        place_ref, field_ref, *refs = refs
    count = len(sources)
    targets, sems = refs[:count], refs[-1]
    gathered = targets if on_chip else [refs[count].at[which] for which in range(count)]
    columns = targets[0].shape[1]
    reads, writes = [], []
    for which, source in enumerate(sources):
        at = pl.multiple_of(source(0, place_ref) * unit, unit)
        reads.append(
            pltpu.make_async_copy(
                field_ref.at[:, pl.ds(at, columns)], gathered[which], sems.at[0, which]
            )
        )
        if not on_chip:
            writes.append(
                pltpu.make_async_copy(gathered[which], targets[which], sems.at[1, which])
            )
    for read in reads:
        read.start()
    for which, read in enumerate(reads):
        read.wait()
        if writes:
            writes[which].start()
    for write in writes:
        write.wait()


def pack(field, place, halo, peers, unit, group_units, first, count, groups, on_chip=False):
    hours_dev = field.shape[0]
    last = groups * group_units - 1

    def source_of(peer):
        def source(i, place):
            group = place[peer]
            start = jnp.where(ascends(group), first, group_units - first - count)
            return group * group_units + start + i

        return source

    sources = [source_of(peer) for peer in peers]

    def spec(source):
        return pl.BlockSpec(
            (hours_dev, unit), lambda i, place: (0, jnp.clip(source(i, place), 0, last))
        )

    bytes_moved = 4 * len(peers) * hours_dev * count * unit
    if halo is None:
        shape = (hours_dev, count * unit)
        kind = pltpu.VMEM if on_chip else jax.ShapeDtypeStruct
        space = pltpu.VMEM if on_chip else pl.ANY
        scratch = [] if on_chip else [pltpu.VMEM((len(peers),) + shape, field.dtype)]
        operands = [field] if on_chip else [place, field]
        return pl.pallas_call(
            functools.partial(copy_kernel, unit, sources, peers, on_chip),
            out_shape=[kind(shape, field.dtype) for _ in peers],
            grid_spec=pltpu.PrefetchScalarGridSpec(
                num_scalar_prefetch=len(operands) - 1,
                grid=(),
                in_specs=[pl.BlockSpec(memory_space=pl.ANY)],
                out_specs=[pl.BlockSpec(memory_space=space) for _ in peers],
                scratch_shapes=scratch + [pltpu.SemaphoreType.DMA((2, len(peers)))],
            ),
            cost_estimate=pl.CostEstimate(
                flops=0, transcendentals=0, bytes_accessed=bytes_moved
            ),
            name="pack",
        )(*operands)
    in_specs = [spec(source) for source in sources]
    operands = [field] * len(peers)
    in_specs += [pl.BlockSpec((hours_dev, unit), lambda i, place: (0, 0))] * 2
    operands += list(halo)
    return pl.pallas_call(
        functools.partial(pack_kernel, last, sources),
        out_shape=[jax.ShapeDtypeStruct((hours_dev, count * unit), field.dtype) for _ in peers],
        grid_spec=pltpu.PrefetchScalarGridSpec(
            num_scalar_prefetch=1,
            grid=(count,),
            in_specs=in_specs,
            out_specs=[pl.BlockSpec((hours_dev, unit), lambda i, place: (0, i)) for _ in peers],
        ),
        cost_estimate=pl.CostEstimate(
            flops=0,
            transcendentals=0,
            bytes_accessed=bytes_moved,
        ),
        name="pack",
    )(place, *operands)


def rows_kernel(place_ref, source, target):
    target[...] = source[...]


def order_rows(temporal_cov, place, groups):
    hours_all = temporal_cov.shape[0]
    hours_dev = hours_all // groups
    return pl.pallas_call(
        rows_kernel,
        out_shape=jax.ShapeDtypeStruct(temporal_cov.shape, temporal_cov.dtype),
        grid_spec=pltpu.PrefetchScalarGridSpec(
            num_scalar_prefetch=1,
            grid=(groups,),
            in_specs=[pl.BlockSpec((hours_dev, hours_all), lambda i, place: (place[i], 0))],
            out_specs=pl.BlockSpec((hours_dev, hours_all), lambda i, place: (i, 0)),
        ),
        name="order",
    )(place, temporal_cov)


def product_kernel(cfg, place_ref, neighbours_ref, counts_ref, cov_ref, *refs):
    groups, unit, block, slots, chunk_units, group_units, first_out, lead = cfg["dims"]
    opening, has_next = cfg["flags"]
    refs = list(refs)
    pieces = [refs.pop(0) for _ in range(groups)]
    inner = [refs.pop(0) for _ in range(groups)] if opening else None
    outset = [refs.pop(0) for _ in range(groups)] if opening else None
    carry_ref = None if opening else refs.pop(0)
    tiles_ref = refs.pop(0)
    outs = [refs.pop(0) for _ in range(groups)]
    final_ref = None if has_next else refs.pop(0)
    next_ref = refs.pop(0) if has_next else None
    panel, mixed, banded = refs

    step = pl.program_id(0)
    steps = pl.num_programs(0)
    upward = ascends(place_ref[0])
    hours_dev = pieces[0].shape[0]
    reach = (slots - 1) // 2
    width = slots + 1

    def columns(position):
        at = jnp.where(upward, position, chunk_units + 1 - position)
        return pl.ds(pl.multiple_of(at * unit, unit), unit)

    @pl.when(step == 0)
    def _():
        for pair in range(banded.shape[0]):
            banded[pair, :block, slots * block :] = jnp.zeros((block, block), banded.dtype)
            banded[pair, block:, :block] = jnp.zeros((block, block), banded.dtype)
        if not opening:
            for which in range(2):
                mixed[:, columns(which)] = carry_ref[:, which * unit : (which + 1) * unit]

    def load(sources):
        for peer in range(groups):
            at = pl.multiple_of(place_ref[peer] * hours_dev, hours_dev)
            panel[pl.ds(at, hours_dev), :] = sources[peer][...]

    if opening:
        pl.when(step == 0)(lambda: load(inner))
        pl.when(step == 1)(lambda: load(outset))
        pl.when(step >= 2)(lambda: load(pieces))
    else:
        load(pieces)

    fresh = jnp.dot(cov_ref[...], panel[...], preferred_element_type=jnp.float32).astype(mixed.dtype)
    mixed[:, columns(step + lead)] = fresh
    if has_next:
        for which in range(2):

            @pl.when(step == steps - 2 + which)
            def _():
                next_ref[:, which * unit : (which + 1) * unit] = fresh

    @pl.when(step + lead >= 2)
    def _():
        turn = step + lead - 2
        at = jnp.where(upward, turn, chunk_units - 1 - turn)
        own_unit = jnp.where(upward, first_out + turn, group_units - 1 - first_out - turn)
        first_row = own_unit * (unit // block)
        base = pl.multiple_of(at * unit, unit)
        for pair in range(unit // block // 2):
            for which in range(2):
                row = 2 * pair + which
                mine = first_row + row
                block_id = place_ref[groups] + mine
                live = counts_ref[mine]
                for slot in range(slots):
                    offset = neighbours_ref[mine, slot] - block_id + (reach + which)
                    offset = jnp.clip(offset, 0, slots)
                    tile = tiles_ref[row, slot]
                    banded[
                        pair,
                        which * block : (which + 1) * block,
                        pl.ds(pl.multiple_of(offset * block, block), block),
                    ] = jnp.where(slot < live, tile, jnp.zeros_like(tile))
            window = mixed[:, pl.ds(pl.multiple_of(base + 2 * pair * block, block), width * block)]
            summed = lax.dot_general(
                window, banded[pair], (((1,), (1,)), ((), ())), preferred_element_type=jnp.float32
            ).astype(outs[0].dtype)
            for peer in range(groups):

                def store(target):
                    target[:, 2 * pair * block : 2 * (pair + 1) * block] = summed[
                        peer * hours_dev : (peer + 1) * hours_dev
                    ]

                if final_ref is not None and peer == groups - 1:
                    pl.when(turn < chunk_units - 1)(lambda: store(outs[-1]))
                    pl.when(turn == chunk_units - 1)(lambda: store(final_ref))
                else:
                    store(outs[peer])


def products(place, neighbours, counts, cov, pieces, start, carry, spatial_blocks, layout, chunk):
    groups, unit, block, slots, group_units, chunk_units = layout
    chunks = group_units // chunk_units
    hours_all, hours_dev = cov.shape[0], pieces[0].shape[0]
    opening, has_next = chunk == 0, chunk < chunks - 1
    lead = 0 if opening else 2
    steps = chunk_units + 2 - lead
    first_out = chunk * chunk_units

    def piece_index(i, place, *_):
        turn = jnp.maximum(i + lead - 2, 0)
        return 0, jnp.where(ascends(place[0]), turn, chunk_units - 1 - turn)

    def tile_index(i, place, *_):
        turn = first_out + jnp.maximum(i + lead - 2, 0)
        return jnp.where(ascends(place[0]), turn, group_units - 1 - turn), 0, 0, 0

    def whole(shape):
        return pl.BlockSpec(shape, lambda i, *_: (0, 0))

    piece_spec = pl.BlockSpec((hours_dev, unit), piece_index)
    in_specs = [whole((hours_all, hours_all))] + [piece_spec] * groups
    operands = [cov] + list(pieces)
    if opening:
        in_specs += [whole((hours_dev, unit))] * (2 * groups)
        operands += list(start[0]) + list(start[1])
    else:
        in_specs += [whole((hours_all, 2 * unit))]
        operands += [carry]
    blocks_unit = unit // block
    in_specs += [pl.BlockSpec((blocks_unit, slots, block, block), tile_index)]
    operands += [spatial_blocks]
    dtype = pieces[0].dtype
    out_shape = [jax.ShapeDtypeStruct((hours_dev, chunk_units * unit), dtype)] * groups
    out_specs = [piece_spec] * groups
    if not has_next:
        def body_index(i, place, *_):
            turn = jnp.clip(i + lead - 2, 0, chunk_units - 2)
            return 0, jnp.where(ascends(place[0]), turn, chunk_units - 2 - turn)

        out_shape = out_shape[:-1] + [
            jax.ShapeDtypeStruct((hours_dev, (chunk_units - 1) * unit), dtype),
            jax.ShapeDtypeStruct((hours_dev, unit), dtype),
        ]
        out_specs = out_specs[:-1] + [
            pl.BlockSpec((hours_dev, unit), body_index),
            whole((hours_dev, unit)),
        ]
    if has_next:
        out_shape += [jax.ShapeDtypeStruct((hours_all, 2 * unit), dtype)]
        out_specs += [whole((hours_all, 2 * unit))]
    cfg = {
        "dims": (groups, unit, block, slots, chunk_units, group_units, first_out, lead),
        "flags": (opening, has_next),
    }
    flops = 2 * hours_all * unit * (steps * hours_all + chunk_units * (slots + 1) * block)
    results = pl.pallas_call(
        functools.partial(product_kernel, cfg),
        out_shape=out_shape,
        grid_spec=pltpu.PrefetchScalarGridSpec(
            num_scalar_prefetch=3,
            grid=(steps,),
            in_specs=in_specs,
            out_specs=out_specs,
            scratch_shapes=[
                pltpu.VMEM((hours_all, unit), dtype),
                pltpu.VMEM((hours_all, (chunk_units + 2) * unit), dtype),
                pltpu.VMEM((blocks_unit // 2, 2 * block, (slots + 1) * block), dtype),
            ],
        ),
        compiler_params=pltpu.CompilerParams(vmem_limit_bytes=48 * MiB),
        cost_estimate=pl.CostEstimate(
            flops=flops,
            transcendentals=0,
            bytes_accessed=2 * hours_all * unit * (steps + chunk_units)
            + 2 * chunk_units * blocks_unit * slots * block * block,
        ),
        name="products",
    )(place, neighbours, counts, *operands)
    return results[:groups], results[groups]


def place_kernel(peers, starts, unit, group_units, on_chip, *refs):
    target, sems = refs[-2], refs[-1]
    if on_chip:
        mine = lax.axis_index("tm")
        place_ref = {peer: jnp.bitwise_xor(mine, peer) for peer in peers}
    else:
        place_ref, *refs = refs
    copies = []
    for which, peer in enumerate(peers):
        source = refs[which]
        columns = source.shape[1]
        group = place_ref[peer]
        at = (group * group_units + jnp.where(ascends(group), *starts)) * unit
        rows = source.shape[0] // ROW_COPIES
        for part in range(ROW_COPIES):
            copies.append(
                pltpu.make_async_copy(
                    source.at[part * rows : (part + 1) * rows],
                    target.at[
                        part * rows : (part + 1) * rows,
                        pl.ds(pl.multiple_of(at, unit), columns),
                    ],
                    sems.at[which, part],
                )
            )
    for copy in copies:
        copy.start()
    for copy in copies:
        copy.wait()


def put(result, pieces, peers, place, cells_dev, starts, unit, group_units, on_chip):
    hours_dev, columns = pieces[0].shape
    in_specs = [pl.BlockSpec(memory_space=pltpu.VMEM)] * len(pieces)
    operands = list(pieces)
    scalars = [] if on_chip else [place]
    if on_chip:
        operands = [pltpu.with_memory_space_constraint(piece, pltpu.VMEM) for piece in pieces]
    aliases = {}
    if result is not None:
        in_specs += [pl.BlockSpec(memory_space=pl.ANY)]
        operands += [result]
        aliases = {len(scalars) + len(pieces): 0}
    return pl.pallas_call(
        functools.partial(place_kernel, peers, starts, unit, group_units, on_chip),
        out_shape=jax.ShapeDtypeStruct((hours_dev, cells_dev), pieces[0].dtype),
        grid_spec=pltpu.PrefetchScalarGridSpec(
            num_scalar_prefetch=len(scalars),
            grid=(),
            in_specs=in_specs,
            out_specs=pl.BlockSpec(memory_space=pl.ANY),
            scratch_shapes=[pltpu.SemaphoreType.DMA((len(pieces), ROW_COPIES))],
        ),
        input_output_aliases=aliases,
        cost_estimate=pl.CostEstimate(
            flops=0, transcendentals=0, bytes_accessed=4 * len(pieces) * hours_dev * columns
        ),
        name="place",
    )(*scalars, *operands)


def per_device(field, temporal_cov, spatial_blocks, neighbours, counts):
    groups = lax.axis_size("tm")
    spaces = lax.axis_size("space")
    _, cells_dev = field.shape
    per_group, slots, block = spatial_blocks.shape[:3]
    reach = (slots - 1) // 2
    unit = reach * block
    group_units = per_group // reach
    chunk_units = CHUNK_UNITS if group_units % CHUNK_UNITS == 0 else group_units
    chunks = group_units // chunk_units
    layout = (groups, unit, block, slots, group_units, chunk_units)

    mine = lax.axis_index("tm")
    first_block = (lax.axis_index("space") * groups + mine) * per_group
    place = jnp.concatenate(
        [
            jnp.bitwise_xor(mine.astype(jnp.int32), jnp.arange(groups, dtype=jnp.int32)),
            first_block.astype(jnp.int32)[None],
        ]
    )

    peers = list(range(groups))

    def swap(array, peer):
        return lax.ppermute(array, "tm", [(at, at ^ peer) for at in range(groups)])

    def swap_all(arrays):
        moved = {peer: swap(arrays[peer], peer) for peer in peers[2:] + peers[1:2]}
        return [arrays[0]] + [moved[peer] for peer in range(1, groups)]

    forward = [(at, at + 1) for at in range(spaces - 1)]
    backward = [(to, at) for at, to in forward]

    far = pack(field, None, None, peers[2:], unit, group_units, 0, 1, groups, True)
    near = pack(field, None, None, peers[:2], unit, group_units, 0, 1, groups, True)
    first_sent = near + far
    first = swap_all(first_sent)
    low = lax.ppermute(field[:, cells_dev - unit :], "space", forward)
    high = lax.ppermute(field[:, :unit], "space", backward)
    arrived, sent = [], first_sent
    for chunk in range(chunks):
        halo = (low, high) if chunk == chunks - 1 else None
        turn, _ = lax.optimization_barrier((place, sent[-1]))
        sent = pack(
            field, turn, halo, peers, unit, group_units,
            1 + chunk * chunk_units, chunk_units, groups,
        )
        arrived.append(swap_all(sent))
    inner = [first_sent[1]] + [swap(first[peer ^ 1], 1) for peer in range(1, groups)]
    cov = order_rows(temporal_cov, place, groups)
    carry, result = None, None
    returned = []
    for chunk in range(chunks):
        outs, carry = products(
            place, neighbours, counts, cov, arrived[chunk], (inner, first), carry,
            spatial_blocks, layout, chunk,
        )
        returned.append(swap_all(outs))
    final = swap(carry, groups - 1)
    for chunk in range(chunks):
        closing = chunk == chunks - 1
        up, down = chunk * chunk_units, group_units - (chunk + 1) * chunk_units
        parts = [(peers, (up, down))]
        if closing:
            parts = [(peers[:2], (up, down)), (peers[2:-1], (up, down)), (peers[-1:], (up, down + 1))]
        for part, (listed, starts) in enumerate(parts):
            result = put(
                result, [returned[chunk][peer] for peer in listed], listed, place,
                cells_dev, starts, unit, group_units, closing and part > 0,
            )
    starts = (group_units - 1, 0)
    result = put(result, [final], peers[-1:], place, cells_dev, starts, unit, group_units, True)
    return result


def solution(mesh):
    placed = (
        P("tm", "space"),
        P(),
        P(("space", "tm"), None, None, None),
        P(("space", "tm"), None),
        P(("space", "tm")),
    )
    return jax.shard_map(
        per_device, mesh=mesh, in_specs=placed, out_specs=P("tm", "space"), check_vma=False
    )
```
